128 devices in a mesh: gx: 8 (over x, core), gy: 16 (over y, z).
Axes of the slice: x: 4, y: 4, z: 4, core: 2. Of those that a mesh axis runs over, the one named last changes fastest.
Arguments:
- emission: bfloat16 [393216, 128], P(('gx', 'gy')), may hold values from -6 to 6
- reflectance: float32 [393216], P(('gx', 'gy')), may hold values from 0.3 to 0.9
- link_blocks: bfloat16 [18432, 256, 256], P(('gx', 'gy')), may hold values from -0.109375 to 0.109375
- link_source: int32 [18432], P(('gx', 'gy')), may hold values from 0 to 11
- link_target: int32 [18432, 1], P(('gx', 'gy')), may hold values from 0 to 127, as said below
- link_slot: int32 [18432], P(('gx', 'gy')), may hold values from 0 to 11
- sensor_cell: int32 [65536, 8], P(('gx', 'gy')), may hold values from 0 to 9215
- sensor_weight: float32 [65536, 8], P(('gx', 'gy')), may hold values from 0 to 0.25
Outputs:
- radiosity: float32 [393216, 128], P(('gx', 'gy'))
- sensor_values: float32 [65536, 128], P(('gx', 'gy'))
The draws below stay inside these ranges and needn't reach their ends.
Inputs may be any that keep to these rules, and one draw needn't show every extreme that they name: `link_target`: the owner of each block is the device that holds it or one of that device's neighbours (i +- 1, j) or (i, j +- 1) inside the grid of devices, without wrapping. Among the 144 blocks of one device at most 9 name any one neighbour, and some neighbour is named exactly 9 times.
All inputs are finite; a program needn't handle non-finite values.
Results may differ from the reference program's by a relative error of at most 0.0039.
Values may be sent and summed in bfloat16 or wider, within the bound.
No kernel may reach another device: no remote copies, remote signals or barrier semaphores. Data moves between devices by JAX's collectives and lax.ppermute only.
A program may use at most 128 MiB of HBM per device.

```python
import jax
import jax.numpy as jnp
from jax import lax

P_SIZE = 256
S = 128
CL_DEV = 12
LINKS = 12
SWEEPS = 2
SENS_DEV = 512
TAPS = 8
CLUSTERS = 1536
LINK_DEV = 144
LINKS_ALL = 18432
CAP = 9
SENSORS = 65536
N_GX = 8
N_GY = 16


def draw_link_target(key, part):
    devices = N_GX * N_GY
    index = jnp.arange(devices, dtype=jnp.int32)
    row = index // N_GY
    col = index % N_GY
    exists = jnp.stack([row + 1 < N_GX, row >= 1, col + 1 < N_GY, col >= 1], axis=1).astype(jnp.int32)
    owners = jnp.stack([index + N_GY, index - N_GY, index + 1, index - 1, index], axis=1)
    first_key, second_key, third_key = jax.random.split(jax.random.fold_in(key, 11), 3)
    lowest = max(1, CAP // 2)
    counts = jax.random.randint(first_key, (devices, 4), lowest, CAP + 1).astype(jnp.int32) * exists
    start = jax.random.randint(second_key, (devices,), 0, 4).astype(jnp.int32)
    order = (start[:, None] + jnp.arange(4, dtype=jnp.int32)[None, :]) % 4
    exists_turned = jnp.take_along_axis(exists, order, axis=1)
    first = jnp.argmax(exists_turned, axis=1).astype(jnp.int32)
    picked = jnp.take_along_axis(order, first[:, None], axis=1)[:, 0]
    counts = jnp.where(jnp.arange(4, dtype=jnp.int32)[None, :] == picked[:, None], CAP, counts)
    edges = jnp.cumsum(counts, axis=1)
    position = jnp.arange(LINK_DEV, dtype=jnp.int32)
    label = jnp.sum((position[None, :, None] >= edges[:, None, :]).astype(jnp.int32), axis=2)
    target = jnp.take_along_axis(owners, label, axis=1)
    scores = jax.random.randint(third_key, (devices, LINK_DEV), 0, 1 << 20).astype(jnp.int32) * LINK_DEV + position[None, :]
    shuffle = jnp.argsort(scores, axis=1)
    target = jnp.take_along_axis(target, shuffle, axis=1)
    return target.reshape(devices * LINK_DEV, 1).astype(jnp.int32)


def place_ends(drawn, key, smallest, high):
    longest = drawn.shape.index(max(drawn.shape))
    spots = []
    for shift in (0, 1):
        where = [jax.random.randint(jax.random.fold_in(key, axis), (), 0, length) for axis, length in enumerate(drawn.shape)]
        where[longest] = (where[longest] + shift) % drawn.shape[longest]
        spots.append(tuple(where))
    return drawn.at[spots[0]].set(smallest).at[spots[1]].set(high)


def shard_levels(key, extent, cuts, smallest, largest):
    factor_of, own = 1.0, jax.random.fold_in(key, 6)
    for dim, shards_of in cuts:
        heights = jnp.exp(jax.random.uniform(jax.random.fold_in(own, dim), (shards_of,), jnp.float32, smallest / len(cuts), largest / len(cuts)))
        factor_of = factor_of * jnp.repeat(heights, extent[dim] // shards_of).reshape([-1 if axis == dim else 1 for axis in range(len(extent))])
    return factor_of


def centred(key, dims, spread, bound, shards=(), kind=jnp.bfloat16):
    gain = shard_levels(key, dims, shards, -0.22, 0.18) if shards else 1.0
    array = jax.random.normal(key, dims, jnp.float32) * spread * gain
    return jnp.minimum(jnp.maximum(array, -bound), bound).astype(kind)


def setup_inputs(seed: int = 0) -> dict:
    arg_keys = jax.random.split(jax.random.key(seed), 9)
    emission = centred(arg_keys[0], (CLUSTERS * P_SIZE, S), 1.0, 6.0, ((0, 128),))
    reflectance = jnp.clip(0.3 + 0.59999996 * jax.random.uniform(arg_keys[1], (CLUSTERS * P_SIZE,), jnp.float32) ** shard_levels(arg_keys[1], (CLUSTERS * P_SIZE,), ((0, 128),), -0.2, 0.2), 0.3, 0.9)
    link_blocks = centred(arg_keys[2], (LINKS_ALL, P_SIZE, P_SIZE), (P_SIZE * LINKS) ** -0.5, 0.109375, ((0, 128),))
    link_source = place_ends(jax.random.randint(arg_keys[3], (LINKS_ALL,), 0, CL_DEV), jax.random.fold_in(arg_keys[3], 1), 0, CL_DEV - 1).astype(jnp.int32)
    link_target = draw_link_target(jax.random.fold_in(arg_keys[8], 71), 0)
    link_slot = place_ends(jax.random.randint(arg_keys[5], (LINKS_ALL,), 0, CL_DEV), jax.random.fold_in(arg_keys[5], 1), 0, CL_DEV - 1).astype(jnp.int32)
    sensor_cell = place_ends(jax.random.randint(arg_keys[6], (SENSORS, TAPS), 0, 3 * CL_DEV * P_SIZE), jax.random.fold_in(arg_keys[6], 1), 0, (3 * CL_DEV * P_SIZE) - 1).astype(jnp.int32)
    sensor_weight = jnp.clip(0.25 * jax.random.uniform(arg_keys[7], (SENSORS, TAPS), jnp.float32) ** shard_levels(arg_keys[7], (SENSORS, TAPS), ((0, 128),), -0.2, 0.2), 0.0, 0.25)
    return {"emission": emission, "reflectance": reflectance, "link_blocks": link_blocks, "link_source": link_source, "link_target": link_target, "link_slot": link_slot, "sensor_cell": sensor_cell, "sensor_weight": sensor_weight}


def reference(emission, reflectance, link_blocks, link_source, link_target, link_slot, sensor_cell, sensor_weight):
    devices = N_GX * N_GY
    clusters = CL_DEV * devices
    base = emission.astype(jnp.float32)
    blocks = link_blocks.reshape(devices, LINK_DEV, P_SIZE, P_SIZE)
    offsets = (CL_DEV * jnp.arange(devices, dtype=jnp.int32))[:, None]
    sources = (link_source.reshape(devices, LINK_DEV) + offsets).astype(jnp.int32)
    targets = (link_target[:, 0] * CL_DEV + link_slot).reshape(devices, LINK_DEV).astype(jnp.int32)
    radiosity = base
    for sweep in range(SWEEPS):
        rounded = radiosity.astype(jnp.bfloat16)
        rounded = lax.optimization_barrier(rounded).astype(jnp.float32).reshape(clusters, P_SIZE, S)

        def step(incoming, item):
            block, source, target = item
            term = jnp.einsum("lpq,lqs->lps", block.astype(jnp.float32), rounded[source],
                              precision=lax.Precision.HIGHEST).astype(jnp.bfloat16)
            term = lax.optimization_barrier(term).astype(jnp.float32)
            return incoming.at[target].add(term), None

        incoming, _ = lax.scan(step, jnp.zeros((clusters, P_SIZE, S), jnp.float32), (blocks, sources, targets))
        radiosity = base + reflectance[:, None] * incoming.reshape(clusters * P_SIZE, S)
    rows = CL_DEV * P_SIZE
    final = radiosity.astype(jnp.bfloat16).reshape(N_GX, N_GY, rows, S)
    padded = jnp.pad(final, ((0, 0), (1, 1), (0, 0), (0, 0))).reshape(-1, S)
    device_of = (jnp.arange(SENS_DEV * devices, dtype=jnp.int32) // SENS_DEV).astype(jnp.int32)
    row_index = (device_of // N_GY).astype(jnp.int32)
    col_index = (device_of % N_GY).astype(jnp.int32)
    which = sensor_cell // rows
    within = sensor_cell % rows
    flat = ((row_index[:, None] * (N_GY + 2) + col_index[:, None] + which) * rows + within).astype(jnp.int32)
    sensor_values = jnp.zeros((SENS_DEV * devices, S), jnp.float32)
    for tap in range(TAPS):
        sensor_values = sensor_values + sensor_weight[:, tap][:, None] * padded[flat[:, tap]].astype(jnp.float32)
    return radiosity, sensor_values
```

```python
import functools

import jax
import jax.numpy as jnp
from jax import lax
from jax.experimental import pallas as pl
from jax.experimental.pallas import tpu as pltpu
from jax.sharding import PartitionSpec as P

BF16, F32, I32, I16 = jnp.bfloat16, jnp.float32, jnp.int32, jnp.int16
P_SIZE = 256
S = 128
CL = 12
SENS = 512
TAPS = 8
LINKS = 144
CAP = 9
ROWS = CL * P_SIZE
TERM_ROWS = CAP * P_SIZE
SLOT_ROWS = 16
META_ROWS = 3 * TAPS * SENS // S
GX_ROWS = TERM_ROWS + SLOT_ROWS
GY_ROWS = GX_ROWS + META_ROWS
OWN_PAD = LINKS + 16
GROUP = 16
MIB = 1 << 20

VM = pl.BlockSpec(memory_space=pltpu.VMEM)
SM = pl.BlockSpec(memory_space=pltpu.SMEM)
ANY = pl.BlockSpec(memory_space=pl.ANY)

PAIR = 2 * CAP
SPARE = 3 * PAIR
OWN_SRC, OWN_AIM, OWN_COUNT = OWN_PAD, 2 * OWN_PAD, 3 * OWN_PAD
CHUNK = 16


def params(mib):
    return pltpu.CompilerParams(vmem_limit_bytes=mib * MIB)


def on_chip(x):
    return pltpu.with_memory_space_constraint(x, pltpu.VMEM)


def partners(n_cols):
    i, j = lax.axis_index("gx"), lax.axis_index("gy")
    here = i * n_cols + j
    step_y, step_x = 1 - 2 * (j % 2), 1 - 2 * (i % 2)
    return here, (
        here + step_y,
        here - step_y,
        here + step_x * n_cols,
        here - step_x * n_cols,
    )


def dot(a, b):
    return jnp.dot(a, b, preferred_element_type=F32)


def in_hbm(x):
    return pltpu.with_memory_space_constraint(x, pltpu.HBM)


def settle(tab, counts, source, slot):
    for p in range(PAIR):
        filled = p % CAP < counts[p // CAP]
        link = jnp.where(filled, tab[p], 0)
        tab[p] = link
        tab[PAIR + p] = source[link]
        tab[2 * PAIR + p] = jnp.where(filled, slot[link] + 1, 0)


def fetch(tab, blocks, buf, sems):
    copies = [pltpu.make_async_copy(blocks.at[tab[p]], buf.at[p], sems.at[p]) for p in range(PAIR)]
    for copy in copies:
        copy.start()
    return copies


def send_terms(tab, block, field, packs):
    for p in range(PAIR):
        term = jnp.where(tab[2 * PAIR + p] > 0, dot(block(p), field[tab[PAIR + p]]), 0.0)
        packs[p // CAP][pl.ds((p % CAP) * P_SIZE, P_SIZE), :] = term.astype(BF16)


def put_slots(tab, packs):
    row = lax.broadcasted_iota(I32, (SLOT_ROWS, S), 0)
    for side in range(2):
        slots = jnp.zeros((SLOT_ROWS, S), I32)
        for k in range(CAP):
            slots = jnp.where(row == k, tab[2 * PAIR + side * CAP + k], slots)
        packs[side][pl.ds(TERM_ROWS, SLOT_ROWS), :] = slots.astype(F32).astype(BF16)


def sensor_rows(cells, weights, weights_sum, packs):
    cell, weight = cells[...], weights[...]
    total = weight
    for shift in range(1, TAPS):
        same = pltpu.roll(cell, shift, 0) == cell
        total = total + jnp.where(same, pltpu.roll(weight, shift, 0), 0.0)
    weights_sum[...] = total
    meta = []
    for part in ((cell >> 7).astype(F32), (cell & 127).astype(F32), total):
        for q in range(SENS // S):
            meta.append(part[:, q * S : (q + 1) * S])
    meta = jnp.concatenate(meta, axis=0).astype(BF16)
    for pack in packs:
        pack[pl.ds(GX_ROWS, META_ROWS), :] = meta


def first_kernel(
    n_cols, target, source, slot, emission, blocks, cells, weights,
    pack_e, pack_o, tab, weights_sum, field, buf, sems, sem_field,
):
    field_copy = pltpu.make_async_copy(emission, field, sem_field)
    field_copy.start()
    gy_e, gy_o, _, _ = partners(n_cols)[1]

    def scan(link, counts):
        owner = target[0, link]
        even, odd = owner == gy_e, owner == gy_o
        tab[jnp.where(even, counts[0], jnp.where(odd, CAP + counts[1], SPARE))] = link
        return counts[0] + even.astype(I32), counts[1] + odd.astype(I32)

    counts = lax.fori_loop(0, LINKS, scan, (jnp.int32(0),) * 2, unroll=8)
    settle(tab, counts, source, slot)
    copies = fetch(tab, blocks, buf, sems)
    packs = (pack_e, pack_o)
    put_slots(tab, packs)
    sensor_rows(cells, weights, weights_sum, packs)
    field_copy.wait()
    for copy in copies:
        copy.wait()
    send_terms(tab, lambda p: buf[p], field, packs)


def gx_kernel(
    n_cols, target, source, slot, emission, blocks,
    pack_e, pack_o, tab, own, field, buf, sems, sem_field,
):
    field_copy = pltpu.make_async_copy(emission, field, sem_field)
    field_copy.start()
    gy_e, gy_o, gx_e, gx_o = partners(n_cols)[1]

    def scan(link, counts):
        owner = target[0, link]
        even, odd = owner == gx_e, owner == gx_o
        other = even | odd | (owner == gy_e) | (owner == gy_o)
        tab[jnp.where(even, counts[0], jnp.where(odd, CAP + counts[1], SPARE))] = link
        own[counts[2]] = link
        return (
            counts[0] + even.astype(I32),
            counts[1] + odd.astype(I32),
            counts[2] + jnp.where(other, 0, 1),
        )

    counts = lax.fori_loop(0, LINKS, scan, (jnp.int32(0),) * 3, unroll=8)
    settle(tab, counts, source, slot)
    copies = fetch(tab, blocks, buf, sems)
    packs = (pack_e, pack_o)
    put_slots(tab, packs)
    field_copy.wait()
    for copy in copies:
        copy.wait()
    send_terms(tab, lambda p: buf[p], field, packs)
    for k in range(GROUP):
        own[counts[2] + k] = 0
    groups = (counts[2] + GROUP - 1) // GROUP
    own[OWN_COUNT] = groups

    def look_up(n, _):
        link = own[n]
        own[OWN_SRC + n] = source[link]
        own[OWN_AIM + n] = jnp.where(n < counts[2], slot[link], CL)
        return 0

    def look_up_group(g, _):
        for u in range(GROUP):
            look_up(g * GROUP + u, 0)
        return 0

    lax.fori_loop(0, groups, look_up_group, 0)


def own_terms(own, blocks, field, acc, before_group):
    acc[...] = jnp.zeros_like(acc)

    def group(g, state):
        state = before_group(g, state)
        terms = []
        for u in range(GROUP):
            n = g * GROUP + u
            terms.append(dot(blocks[own[n]], field[own[OWN_SRC + n]]).astype(BF16))
        for u in range(GROUP):
            acc[own[OWN_AIM + g * GROUP + u]] += terms[u].astype(F32)
        return state

    return lax.fori_loop(0, own[OWN_COUNT], group, jnp.int32(0))


def own_first_kernel(own, blocks_far, emission, rho, acc, rho_full, blocks, field, sems, sem_field):
    field_copy = pltpu.make_async_copy(emission, field, sem_field)
    field_copy.start()
    chunks = LINKS // CHUNK

    def copy(c):
        part = pl.ds(c * CHUNK, CHUNK)
        return pltpu.make_async_copy(blocks_far.at[part], blocks.at[part], sems.at[c])

    for c in range(chunks):
        copy(c).start()
    for q in range(ROWS // S):
        wide = jnp.broadcast_to(rho[pl.ds(q, 1), :], (S, S))
        rho_full[pl.ds(q * S, S), :] = wide.T
    field_copy.wait()

    def take(c, _):
        copy(c).wait()
        return 0

    def before_group(g, waited):
        last = jnp.where(g + 1 == own[OWN_COUNT], LINKS - 1, own[g * GROUP + GROUP - 1])
        needed = jnp.maximum(waited, (last >> 4) + 1)
        lax.fori_loop(waited, needed, take, 0)
        return needed

    waited = own_terms(own, blocks, field, acc, before_group)
    lax.fori_loop(waited, chunks, take, 0)


def own_kernel(own, blocks, field, acc):
    own_terms(own, blocks, field, acc, lambda g, state: state)


def slots_of(arrived):
    out = []
    for ref in arrived:
        values = ref[pl.ds(TERM_ROWS, SLOT_ROWS), :].astype(F32).astype(I32)
        for k in range(CAP):
            value = values[k, 0]
            out.append(jnp.where(value == 0, CL, value - 1))
    return out


def add_arrived(aims, arrived, acc):
    for n, aim in enumerate(aims):
        rows = pl.ds((n % CAP) * P_SIZE, P_SIZE)
        acc[aim] += arrived[n // CAP][rows, :].astype(F32)


def radiosity_of(emission, rho_full, acc, c):
    rows = pl.ds(c * P_SIZE, P_SIZE)
    return emission[rows, :].astype(F32) + rho_full[rows, :] * acc[c]


def second_kernel(
    tab_y, tab_x, blocks, emission, rho_full, acc_in, gy_e, gy_o, gx_e, gx_o,
    out_gy_e, out_gy_o, out_gx_e, out_gx_o, field, aims_out, acc, base, sem_base,
):
    del acc_in
    base_copy = pltpu.make_async_copy(emission, base, sem_base)
    base_copy.start()
    arrived = (gy_e, gy_o, gx_e, gx_o)
    aims = slots_of(arrived)
    for n, aim in enumerate(aims):
        aims_out[n] = aim
    add_arrived(aims, arrived, acc)
    base_copy.wait()
    for c in range(CL):
        field[c] = radiosity_of(base, rho_full, acc, c).astype(BF16)
    send_terms(tab_y, lambda p: blocks[tab_y[p]], field, (out_gy_e, out_gy_o))
    send_terms(tab_x, lambda p: blocks[tab_x[p]], field, (out_gx_e, out_gx_o))


def spread(cell_rows, weight_rows, out):
    tile, steps = 16, 8
    for q in range(SENS // S):
        cells = [jnp.broadcast_to(cell_rows(k, q), (tile, S)).astype(I16) for k in range(TAPS)]
        weights = [jnp.broadcast_to(weight_rows(k, q), (tile, S)).astype(BF16) for k in range(TAPS)]

        def fill(n, first):
            for m in range(steps):
                here = first + jnp.asarray(m * tile, I16)
                value = jnp.zeros((tile, S), BF16)
                for k in range(TAPS):
                    value = jnp.where(cells[k] == here, weights[k], value)
                start = pl.multiple_of((n * steps + m) * tile, tile)
                out[pl.ds(start, tile), pl.ds(q * S, S)] = value
            return first + jnp.asarray(steps * tile, I16)

        first = lax.broadcasted_iota(I32, (tile, S), 0).astype(I16)
        lax.fori_loop(0, ROWS // (steps * tile), fill, first)


def spread_own_kernel(cells, weights, out):
    spread(
        lambda k, q: cells[pl.ds(k, 1), pl.ds(q * S, S)] - ROWS,
        lambda k, q: weights[pl.ds(k, 1), pl.ds(q * S, S)],
        out,
    )


def spread_pair_kernel(n_cols, gy_e, gy_o, out_e, out_o):
    here, (even, odd, _, _) = partners(n_cols)
    blocks = SENS // S * TAPS
    for partner, arrived, out in ((even, gy_e, out_e), (odd, gy_o, out_o)):
        base = jnp.where(partner > here, 0, 2 * ROWS)
        high = arrived[pl.ds(GX_ROWS, blocks), :].astype(F32).astype(I32)
        low = arrived[pl.ds(GX_ROWS + blocks, blocks), :].astype(F32).astype(I32)
        weight = arrived[pl.ds(GX_ROWS + 2 * blocks, blocks), :].astype(F32)
        cell = high * 128 + low - base
        spread(
            lambda k, q: cell[q * TAPS + k : q * TAPS + k + 1, :],
            lambda k, q: weight[q * TAPS + k : q * TAPS + k + 1, :],
            out,
        )


def final_kernel(
    emission, rho_full, aims, acc_in, gy_e, gy_o, gx_e, gx_o, mix_e, mix_o, mix_own,
    radiosity, part_e, part_o, turned, acc, base, sem_base, sems,
):
    del acc_in, mix_own
    base_copy = pltpu.make_async_copy(emission, base, sem_base)
    base_copy.start()
    add_arrived([aims[n] for n in range(4 * CAP)], (gy_e, gy_o, gx_e, gx_o), acc)
    base_copy.wait()
    copies = []
    for c in range(CL):
        value = radiosity_of(base, rho_full, acc, c)
        acc[c] = value
        copy = pltpu.make_async_copy(acc.at[c], radiosity.at[pl.ds(c * P_SIZE, P_SIZE)], sems.at[c])
        copy.start()
        copies.append(copy)
        turned[:, pl.ds(c * P_SIZE, P_SIZE)] = value.T.astype(BF16)
    part_e[...] = dot(turned[...], mix_e[...]).astype(BF16)
    part_o[...] = dot(turned[...], mix_o[...]).astype(BF16)
    for copy in copies:
        copy.wait()


def own_sensor_kernel(turned, mix, out):
    out[...] = dot(turned[...], mix[...])


def last_kernel(own, part_e, part_o, out):
    total = own[...] + part_e[...].astype(F32) + part_o[...].astype(F32)
    out[...] = total.T


def swap(x, axis, odd):
    size = lax.axis_size(axis)
    pairs = [(i, i + 1) for i in range(odd, size - 1, 2)]
    return lax.ppermute(x, axis, [p for a, b in pairs for p in ((a, b), (b, a))])


def exchange(gy_e, gy_o, gx_e, gx_o):
    sent = (swap(gy_e, "gy", 0), swap(gy_o, "gy", 1), swap(gx_e, "gx", 0), swap(gx_o, "gx", 1))
    return [on_chip(x) for x in sent]


def per_device(
    emission, reflectance, link_blocks, link_source, link_target, link_slot, sensor_cell, sensor_weight
):
    n_cols = lax.axis_size("gy")
    cells, weights = in_hbm(sensor_cell.T), in_hbm(sensor_weight.T)
    flat = in_hbm(emission)
    cube = in_hbm(emission.reshape(CL, P_SIZE, S))
    far = in_hbm(link_blocks)
    links = [in_hbm(x) for x in (link_target.T, link_source, link_slot)]
    one_sem = pltpu.SemaphoreType.DMA
    field_shape = pltpu.VMEM((CL, P_SIZE, S), BF16)
    term_scratch = [
        field_shape,
        pltpu.VMEM((PAIR, P_SIZE, P_SIZE), BF16),
        pltpu.SemaphoreType.DMA((PAIR,)),
        one_sem,
    ]
    base_scratch = [pltpu.VMEM((ROWS, S), BF16), one_sem]
    acc_shape = pltpu.VMEM((CL + 1, P_SIZE, S), F32)
    mix_shape = pltpu.VMEM((ROWS, SENS), BF16)

    def pack_shapes(rows):
        return [pltpu.VMEM((rows, S), BF16)] * 2

    def table(size):
        return jax.ShapeDtypeStruct((size,), I32)

    out_gy_e, out_gy_o, tab_y, weights_sum = pl.pallas_call(
        functools.partial(first_kernel, n_cols),
        out_shape=pack_shapes(GY_ROWS) + [table(128), pltpu.VMEM((TAPS, SENS), F32)],
        in_specs=[SM, SM, SM, ANY, ANY, VM, VM],
        out_specs=[VM, VM, SM, VM],
        scratch_shapes=term_scratch,
        compiler_params=params(16),
        name="gy_terms",
    )(*links, cube, far, cells, weights)
    out_gx_e, out_gx_o, tab_x, own = pl.pallas_call(
        functools.partial(gx_kernel, n_cols),
        out_shape=pack_shapes(GX_ROWS) + [table(128), table(512)],
        in_specs=[SM, SM, SM, ANY, ANY],
        out_specs=[VM, VM, SM, SM],
        scratch_shapes=term_scratch,
        compiler_params=params(16),
        name="gx_terms",
    )(*links, cube, far)
    arrived = exchange(out_gy_e, out_gy_o, out_gx_e, out_gx_o)
    acc, rho_full, near = pl.pallas_call(
        own_first_kernel,
        out_shape=[acc_shape, pltpu.VMEM((ROWS, S), F32), pltpu.VMEM(link_blocks.shape, BF16)],
        in_specs=[SM, ANY, ANY, VM],
        out_specs=[VM, VM, VM],
        scratch_shapes=[field_shape, pltpu.SemaphoreType.DMA((LINKS // CHUNK,)), one_sem],
        compiler_params=params(16),
        name="own_first",
    )(own, far, cube, reflectance.reshape(ROWS // S, S))
    near, rho_full = on_chip(near), on_chip(rho_full)
    mix_own = pl.pallas_call(
        spread_own_kernel,
        out_shape=mix_shape,
        in_specs=[VM, VM],
        out_specs=VM,
        compiler_params=params(16),
        name="spread_own",
    )(cells, on_chip(weights_sum))

    *sent, field, aims, _ = pl.pallas_call(
        second_kernel,
        out_shape=pack_shapes(TERM_ROWS) * 2 + [field_shape, table(4 * CAP), acc_shape],
        in_specs=[SM, SM, VM, ANY] + [VM] * 6,
        out_specs=[VM] * 5 + [SM, VM],
        input_output_aliases={5: 6},
        scratch_shapes=base_scratch,
        compiler_params=params(16),
        name="second_terms",
    )(tab_y, tab_x, near, flat, rho_full, on_chip(acc), *arrived)
    mix_e, mix_o = pl.pallas_call(
        functools.partial(spread_pair_kernel, n_cols),
        out_shape=[mix_shape] * 2,
        in_specs=[VM, VM],
        out_specs=[VM, VM],
        compiler_params=params(16),
        name="spread_pair",
    )(*arrived[:2])
    arrived = exchange(*sent)
    acc = pl.pallas_call(
        own_kernel,
        out_shape=acc_shape,
        in_specs=[SM, VM, VM],
        out_specs=VM,
        compiler_params=params(16),
        name="own_second",
    )(own, near, on_chip(field))

    radiosity, part_e, part_o, turned, _ = pl.pallas_call(
        final_kernel,
        out_shape=[jax.ShapeDtypeStruct((ROWS, S), F32)]
        + [pltpu.VMEM((S, SENS), BF16)] * 2
        + [pltpu.VMEM((S, ROWS), BF16), acc_shape],
        in_specs=[ANY, VM, SM] + [VM] * 7 + [ANY],
        out_specs=[ANY] + [VM] * 4,
        input_output_aliases={3: 4},
        scratch_shapes=base_scratch + [pltpu.SemaphoreType.DMA((CL,))],
        compiler_params=params(16),
        name="final_sum",
    )(
        flat, rho_full, aims, on_chip(acc), *arrived, on_chip(mix_e), on_chip(mix_o), on_chip(mix_own)
    )
    part_e, part_o = swap(part_e, "gy", 0), swap(part_o, "gy", 1)
    own_sum = pl.pallas_call(
        own_sensor_kernel,
        out_shape=pltpu.VMEM((S, SENS), F32),
        in_specs=[VM, VM],
        out_specs=VM,
        compiler_params=params(16),
        name="own_sensors",
    )(on_chip(turned), on_chip(mix_own))
    sensor_values = pl.pallas_call(
        last_kernel,
        out_shape=jax.ShapeDtypeStruct((SENS, S), F32),
        in_specs=[VM, VM, VM],
        out_specs=VM,
        compiler_params=params(16),
        name="sensor_sum",
    )(on_chip(own_sum), on_chip(part_e), on_chip(part_o))
    return radiosity, sensor_values


def solution(mesh):
    spread_axes = P(("gx", "gy"))
    rows = P(("gx", "gy"), None)
    return jax.shard_map(
        per_device,
        mesh=mesh,
        in_specs=(rows, spread_axes, P(("gx", "gy"), None, None), spread_axes, rows, spread_axes, rows, rows),
        out_specs=(rows, rows),
        check_vma=False,
    )
```

```python
import functools

import jax
import jax.numpy as jnp
from jax import lax
from jax.experimental import pallas as pl
from jax.experimental.pallas import tpu as pltpu
from jax.sharding import PartitionSpec as P

BF16, F32, I32, I16 = jnp.bfloat16, jnp.float32, jnp.int32, jnp.int16
P_SIZE = 256
S = 128
CL = 12
SENS = 512
TAPS = 8
LINKS = 144
CAP = 9
ROWS = CL * P_SIZE
TERM_ROWS = CAP * P_SIZE
SLOT_ROWS = 16
META_ROWS = 3 * TAPS * SENS // S
GX_ROWS = TERM_ROWS + SLOT_ROWS
GY_ROWS = GX_ROWS + META_ROWS
PAD = 16
GROUP = 24
OWN_SIZE = 256
MIB = 1 << 20

VM = pl.BlockSpec(memory_space=pltpu.VMEM)
SM = pl.BlockSpec(memory_space=pltpu.SMEM)
ANY = pl.BlockSpec(memory_space=pl.ANY)

PAIR = 2 * CAP
SPARE = 3 * PAIR


def on_chip(x):
    return pltpu.with_memory_space_constraint(x, pltpu.VMEM)


def partners(n_cols):
    i, j = lax.axis_index("gx"), lax.axis_index("gy")
    here = i * n_cols + j
    step_y, step_x = 1 - 2 * (j % 2), 1 - 2 * (i % 2)
    return here, (
        here + step_y,
        here - step_y,
        here + step_x * n_cols,
        here - step_x * n_cols,
    )


def dot(a, b):
    return jnp.dot(a, b, preferred_element_type=F32)


def in_hbm(x):
    return pltpu.with_memory_space_constraint(x, pltpu.HBM)


def in_smem(x):
    return pltpu.with_memory_space_constraint(x, pltpu.SMEM)


def settle(tab, counts, source, slot):
    for p in range(PAIR):
        filled = p % CAP < counts[p // CAP]
        link = jnp.where(filled, tab[p], 0)
        tab[p] = link
        tab[PAIR + p] = source[link]
        tab[2 * PAIR + p] = jnp.where(filled, slot[link] + 1, 0)


def fetch(tab, blocks, buf, sems):
    copies = [pltpu.make_async_copy(blocks.at[tab[p]], buf.at[p], sems.at[p]) for p in range(PAIR)]
    for copy in copies:
        copy.start()
    return copies


def send_terms(tab, block, field, packs, sides=(0, 1)):
    for p in [side * CAP + k for side in sides for k in range(CAP)]:
        term = jnp.where(tab[2 * PAIR + p] > 0, dot(block(p), field[tab[PAIR + p]]), 0.0)
        packs[p // CAP][pl.ds((p % CAP) * P_SIZE, P_SIZE), :] = term.astype(BF16)


def clear_tail(pack, used):
    for row in range(used, pack.shape[0], PAD):
        pack[pl.ds(row, PAD), :] = jnp.zeros((PAD, S), BF16)


def put_slots(tab, packs):
    row = lax.broadcasted_iota(I32, (SLOT_ROWS, S), 0)
    for side in range(2):
        slots = jnp.zeros((SLOT_ROWS, S), I32)
        for k in range(CAP):
            slots = jnp.where(row == k, tab[2 * PAIR + side * CAP + k], slots)
        packs[side][pl.ds(TERM_ROWS, SLOT_ROWS), :] = slots.astype(F32).astype(BF16)


def sensor_rows(cells, weights, weights_sum, packs):
    cell, weight = cells[...], weights[...]
    total = weight
    for shift in range(1, TAPS):
        same = pltpu.roll(cell, shift, 0) == cell
        total = total + jnp.where(same, pltpu.roll(weight, shift, 0), 0.0)
    weights_sum[...] = total
    meta = []
    for part in ((cell >> 7).astype(F32), (cell & 127).astype(F32), total):
        for q in range(SENS // S):
            meta.append(part[:, q * S : (q + 1) * S])
    meta = jnp.concatenate(meta, axis=0).astype(BF16)
    for pack in packs:
        pack[pl.ds(GX_ROWS, META_ROWS), :] = meta


def first_kernel(
    n_cols, target_far, source_far, slot_far, emission, blocks, cells_far, weights_far,
    pack_e, pack_o, tab, weights_sum, target, source, slot, field, cells,
    buf, weights, sems, sem_field, sem_links, sem_sensors,
):
    link_copies = [
        pltpu.make_async_copy(far, near, sem_links.at[n])
        for n, (far, near) in enumerate(
            ((target_far, target), (source_far, source), (slot_far, slot))
        )
    ]
    sensor_copies = [
        pltpu.make_async_copy(cells_far, cells, sem_sensors.at[0]),
        pltpu.make_async_copy(weights_far, weights, sem_sensors.at[1]),
    ]
    field_copy = pltpu.make_async_copy(emission, field, sem_field)
    for copy in (*link_copies, *sensor_copies, field_copy):
        copy.start()
    gy_e, gy_o, _, _ = partners(n_cols)[1]
    for copy in link_copies:
        copy.wait()

    def scan(link, counts):
        owner = target[0, link]
        even, odd = owner == gy_e, owner == gy_o
        tab[jnp.where(even, counts[0], jnp.where(odd, CAP + counts[1], SPARE))] = link
        return counts[0] + even.astype(I32), counts[1] + odd.astype(I32)

    counts = lax.fori_loop(0, LINKS, scan, (jnp.int32(0),) * 2, unroll=8)
    settle(tab, counts, source, slot)
    copies = fetch(tab, blocks, buf, sems)
    packs = (pack_e, pack_o)
    put_slots(tab, packs)
    for copy in sensor_copies:
        copy.wait()
    sensor_rows(cells, weights, weights_sum, packs)
    field_copy.wait()
    clear_tail(pack_o, GY_ROWS)
    for side in range(2):
        for copy in copies[side * CAP : (side + 1) * CAP]:
            copy.wait()
        send_terms(tab, lambda p: buf[p], field, packs, (side,))


def gx_kernel(n_cols, target, source, slot, field, blocks, pack_e, pack_o, tab, own):
    gy_e, gy_o, gx_e, gx_o = partners(n_cols)[1]

    def scan(link, counts):
        owner = target[0, link]
        even, odd = owner == gx_e, owner == gx_o
        other = even | odd | (owner == gy_e) | (owner == gy_o)
        tab[jnp.where(even, counts[0], jnp.where(odd, CAP + counts[1], SPARE))] = link
        own[counts[2]] = link
        return (
            counts[0] + even.astype(I32),
            counts[1] + odd.astype(I32),
            counts[2] + jnp.where(other, 0, 1),
        )

    counts = lax.fori_loop(0, LINKS, scan, (jnp.int32(0),) * 3, unroll=8)
    settle(tab, counts, source, slot)
    packs = (pack_e, pack_o)
    put_slots(tab, packs)
    for k in range(GROUP):
        own[counts[2] + k] = 0
    own[OWN_SIZE - 1] = counts[2]
    send_terms(tab, lambda p: blocks[tab[p]], field, packs)


def gx_second_kernel(tab, blocks, field, pack_e, pack_o):
    send_terms(tab, lambda p: blocks[tab[p]], field, (pack_e, pack_o))


def own_terms(own, source, slot, blocks, field, acc):
    acc[...] = jnp.zeros_like(acc)
    count = own[OWN_SIZE - 1]

    def group(g, _):
        terms = []
        for u in range(GROUP):
            link = own[g * GROUP + u]
            terms.append(dot(blocks[link], field[source[link]]).astype(BF16))
        for u in range(GROUP):
            n = g * GROUP + u
            acc[jnp.where(n < count, slot[own[n]], CL)] += terms[u].astype(F32)
        return 0

    lax.fori_loop(0, (count + GROUP - 1) // GROUP, group, 0)


def own_first_kernel(own, source, slot, blocks, field, rho, acc, rho_full):
    for q in range(ROWS // S):
        wide = jnp.broadcast_to(rho[pl.ds(q, 1), :], (S, S))
        rho_full[pl.ds(q * S, S), :] = wide.T
    own_terms(own, source, slot, blocks, field, acc)


def own_kernel(own, source, slot, blocks, field, acc):
    own_terms(own, source, slot, blocks, field, acc)


def slots_of(arrived):
    out = []
    for ref in arrived:
        values = ref[pl.ds(TERM_ROWS, SLOT_ROWS), :].astype(F32).astype(I32)
        for k in range(CAP):
            value = values[k, 0]
            out.append(jnp.where(value == 0, CL, value - 1))
    return out


def add_arrived(aims, arrived, acc):
    for n, aim in enumerate(aims):
        rows = pl.ds((n % CAP) * P_SIZE, P_SIZE)
        acc[aim] += arrived[n // CAP][rows, :].astype(F32)


def radiosity_of(emission, rho_full, acc, c):
    return emission[c].astype(F32) + rho_full[pl.ds(c * P_SIZE, P_SIZE), :] * acc[c]


def add_slots_kernel(acc_in, first, second, acc, aims_out):
    del acc_in
    aims = slots_of((first, second))
    for n, aim in enumerate(aims):
        aims_out[n] = aim
    add_arrived(aims, (first, second), acc)


def add_kernel(aims, acc_in, first, second, acc):
    del acc_in
    add_arrived([aims[n] for n in range(PAIR)], (first, second), acc)


def second_kernel(
    tab, blocks, emission, rho_full, acc_in, mix_own, gy_e, gy_o,
    pack_e, pack_o, field, aims_out, acc,
):
    del mix_own
    add_slots_kernel(acc_in, gy_e, gy_o, acc, aims_out)
    for c in range(CL):
        field[c] = radiosity_of(emission, rho_full, acc, c).astype(BF16)
    clear_tail(pack_e, TERM_ROWS)
    clear_tail(pack_o, TERM_ROWS)
    send_terms(tab, lambda p: blocks[tab[p]], field, (pack_e, pack_o))


def spread(cell_rows, weight_rows, out):
    tile, steps = 16, 8
    for q in range(SENS // S):
        cells = [jnp.broadcast_to(cell_rows(k, q), (tile, S)).astype(I16) for k in range(TAPS)]
        weights = [jnp.broadcast_to(weight_rows(k, q), (tile, S)).astype(BF16) for k in range(TAPS)]

        def fill(n, first):
            for m in range(steps):
                here = first + jnp.asarray(m * tile, I16)
                value = jnp.zeros((tile, S), BF16)
                for k in range(TAPS):
                    value = jnp.where(cells[k] == here, weights[k], value)
                start = pl.multiple_of((n * steps + m) * tile, tile)
                out[pl.ds(start, tile), pl.ds(q * S, S)] = value
            return first + jnp.asarray(steps * tile, I16)

        first = lax.broadcasted_iota(I32, (tile, S), 0).astype(I16)
        lax.fori_loop(0, ROWS // (steps * tile), fill, first)


def spread_own_kernel(cells, weights, out):
    spread(
        lambda k, q: cells[pl.ds(k, 1), pl.ds(q * S, S)] - ROWS,
        lambda k, q: weights[pl.ds(k, 1), pl.ds(q * S, S)],
        out,
    )


def spread_pair_kernel(n_cols, gy_e, gy_o, out_e, out_o):
    here, (even, odd, _, _) = partners(n_cols)
    blocks = SENS // S * TAPS
    for partner, arrived, out in ((even, gy_e, out_e), (odd, gy_o, out_o)):
        base = jnp.where(partner > here, 0, 2 * ROWS)
        high = arrived[pl.ds(GX_ROWS, blocks), :].astype(F32).astype(I32)
        low = arrived[pl.ds(GX_ROWS + blocks, blocks), :].astype(F32).astype(I32)
        weight = arrived[pl.ds(GX_ROWS + 2 * blocks, blocks), :].astype(F32)
        cell = high * 128 + low - base
        spread(
            lambda k, q: cell[q * TAPS + k : q * TAPS + k + 1, :],
            lambda k, q: weight[q * TAPS + k : q * TAPS + k + 1, :],
            out,
        )


def final_kernel(
    emission, rho_full, aims, acc_in, gy_e, gy_o, mix, radiosity, part, turned, acc
):
    add_kernel(aims, acc_in, gy_e, gy_o, acc)
    for c in range(CL):
        value = radiosity_of(emission, rho_full, acc, c)
        radiosity[pl.ds(c * P_SIZE, P_SIZE), :] = value
        turned[:, pl.ds(c * P_SIZE, P_SIZE)] = value.T.astype(BF16)
    part[...] = dot(turned[...], mix[...]).astype(BF16)


def sensor_kernel(turned, mix, out):
    out[...] = dot(turned[...], mix[...]).astype(out.dtype)


def last_kernel(own, part_e, part_o, out):
    total = own[...] + part_e[...].astype(F32) + part_o[...].astype(F32)
    out[...] = total.T


def swap(x, axis, odd):
    size = lax.axis_size(axis)
    pairs = [(i, i + 1) for i in range(odd, size - 1, 2)]
    return lax.ppermute(x, axis, [p for a, b in pairs for p in ((a, b), (b, a))])


def exchange(axis, even, odd):
    from_odd = swap(odd, axis, 1)
    return [on_chip(swap(even, axis, 0)), on_chip(from_odd)]


def per_device(
    emission, reflectance, link_blocks, link_source, link_target, link_slot, sensor_cell, sensor_weight
):
    n_cols = lax.axis_size("gy")
    sensors_far = in_hbm(sensor_cell.T), in_hbm(sensor_weight.T)
    cube = in_hbm(emission.reshape(CL, P_SIZE, S))
    far, near = in_hbm(link_blocks), on_chip(link_blocks)
    links_far = [in_hbm(x) for x in (link_target.T, link_source, link_slot)]
    field_shape = pltpu.VMEM((CL, P_SIZE, S), BF16)
    acc_shape = pltpu.VMEM((CL + 1, P_SIZE, S), F32)
    mix_shape = pltpu.VMEM((ROWS, SENS), BF16)

    def call(kernel, name, out_shape, in_specs, out_specs, **more):
        return pl.pallas_call(
            kernel,
            out_shape=out_shape,
            in_specs=in_specs,
            out_specs=out_specs,
            compiler_params=pltpu.CompilerParams(vmem_limit_bytes=16 * MIB),
            name=name,
            **more,
        )

    def pack_shapes(even_rows, odd_rows):
        return [pltpu.VMEM((even_rows, S), BF16), pltpu.VMEM((odd_rows, S), BF16)]

    def table(size):
        return pltpu.SMEM((size,), I32)

    out_gy_e, out_gy_o, tab_y, weights_sum, *links, field, cells = call(
        functools.partial(first_kernel, n_cols),
        "gy_terms",
        pack_shapes(GY_ROWS, GY_ROWS + PAD)
        + [table(128), pltpu.VMEM((TAPS, SENS), F32)]
        + [pltpu.SMEM(x.shape, I32) for x in links_far]
        + [field_shape, pltpu.VMEM((TAPS, SENS), I32)],
        [ANY] * 7,
        [VM, VM, SM, VM, SM, SM, SM, VM, VM],
        scratch_shapes=[
            pltpu.VMEM((PAIR, P_SIZE, P_SIZE), BF16),
            pltpu.VMEM((TAPS, SENS), F32),
            pltpu.SemaphoreType.DMA((PAIR,)),
            pltpu.SemaphoreType.DMA,
            pltpu.SemaphoreType.DMA((3,)),
            pltpu.SemaphoreType.DMA((2,)),
        ],
    )(*links_far, cube, far, *sensors_far)
    links, tab_y = [in_smem(x) for x in links], in_smem(tab_y)
    emitted = on_chip(field)
    gy_e, gy_o = exchange("gy", out_gy_e, out_gy_o)
    out_gx_e, out_gx_o, tab_x, own = call(
        functools.partial(gx_kernel, n_cols),
        "gx_terms",
        pack_shapes(GX_ROWS, GX_ROWS) + [table(128), table(OWN_SIZE)],
        [SM, SM, SM, VM, VM],
        [VM, VM, SM, SM],
    )(*links, emitted, near)
    tab_x, own = in_smem(tab_x), in_smem(own)
    gx_e, gx_o = exchange("gx", out_gx_e, out_gx_o)
    acc, rho_full = call(
        own_first_kernel,
        "own_first",
        [acc_shape, pltpu.VMEM((ROWS, S), F32)],
        [SM, SM, SM, VM, VM, VM],
        [VM, VM],
    )(own, *links[1:], near, emitted, reflectance.reshape(ROWS // S, S))
    rho_full = on_chip(rho_full)
    mix_own = call(spread_own_kernel, "spread_own", mix_shape, [VM, VM], VM)(
        on_chip(cells), on_chip(weights_sum)
    )
    mix_own = on_chip(mix_own)
    acc, aims_x = call(
        add_slots_kernel,
        "add_gx_first",
        [acc_shape, table(PAIR)],
        [VM] * 3,
        [VM, SM],
        input_output_aliases={0: 0},
    )(on_chip(acc), gx_e, gx_o)

    out_gy_e, out_gy_o, field, aims_y, _ = call(
        second_kernel,
        "gy_terms_second",
        pack_shapes(TERM_ROWS + PAD, TERM_ROWS + 2 * PAD) + [field_shape, table(PAIR), acc_shape],
        [SM, VM, VM, VM, VM, ANY, VM, VM],
        [VM, VM, VM, SM, VM],
        input_output_aliases={4: 4},
    )(tab_y, near, emitted, rho_full, on_chip(acc), mix_own, gy_e, gy_o)
    field = on_chip(field)
    mix_e, mix_o = call(
        functools.partial(spread_pair_kernel, n_cols), "spread_pair", [mix_shape] * 2, [VM, VM], [VM, VM]
    )(gy_e, gy_o)
    gy_e, gy_o = exchange("gy", out_gy_e, out_gy_o)
    sent = call(
        gx_second_kernel, "gx_terms_second", pack_shapes(TERM_ROWS, TERM_ROWS), [SM, VM, VM], [VM, VM]
    )(tab_x, near, field)
    gx_e, gx_o = exchange("gx", *sent)
    acc = call(own_kernel, "own_second", acc_shape, [SM, SM, SM, VM, VM], VM)(
        own, *links[1:], near, field
    )
    acc = call(
        add_kernel, "add_gx_second", acc_shape, [SM, VM, VM, VM], VM, input_output_aliases={1: 0}
    )(in_smem(aims_x), on_chip(acc), gx_e, gx_o)

    radiosity, part_o, turned, _ = call(
        final_kernel,
        "final_sum",
        [pltpu.VMEM((ROWS, S), F32), pltpu.VMEM((S, SENS), BF16), pltpu.VMEM((S, ROWS), BF16), acc_shape],
        [VM, VM, SM, VM, VM, VM, VM],
        [VM] * 4,
        input_output_aliases={3: 3},
    )(emitted, rho_full, in_smem(aims_y), on_chip(acc), gy_e, gy_o, on_chip(mix_o))
    turned = on_chip(turned)

    def sensor_sums(mix, dtype, name):
        out = call(sensor_kernel, name, pltpu.VMEM((S, SENS), dtype), [VM, VM], VM)(turned, mix)
        return on_chip(out)

    from_o = swap(part_o, "gy", 1)
    from_e = swap(sensor_sums(on_chip(mix_e), BF16, "even_sensors"), "gy", 0)
    sensor_values = call(
        last_kernel, "sensor_sum", jax.ShapeDtypeStruct((SENS, S), F32), [VM, VM, VM], VM
    )(sensor_sums(mix_own, F32, "own_sensors"), on_chip(from_e), on_chip(from_o))
    return radiosity, sensor_values


def solution(mesh):
    spread_axes = P(("gx", "gy"))
    rows = P(("gx", "gy"), None)
    return jax.shard_map(
        per_device,
        mesh=mesh,
        in_specs=(rows, spread_axes, P(("gx", "gy"), None, None), spread_axes, rows, spread_axes, rows, rows),
        out_specs=(rows, rows),
        check_vma=False,
    )
```

```python
import functools

import jax
import jax.numpy as jnp
from jax import lax
from jax.experimental import pallas as pl
from jax.experimental.pallas import tpu as pltpu
from jax.sharding import PartitionSpec as P

BF16, F32, I32, I16 = jnp.bfloat16, jnp.float32, jnp.int32, jnp.int16
P_SIZE = 256
S = 128
CL = 12
SENS = 512
TAPS = 8
LINKS = 144
CAP = 9
ROWS = CL * P_SIZE
TERM_ROWS = CAP * P_SIZE
SLOT_ROWS = 16
META_ROWS = 3 * TAPS * SENS // S
GX_ROWS = TERM_ROWS + SLOT_ROWS
GY_ROWS = GX_ROWS + META_ROWS
PAD = 16
GROUP = 24
OWN_SIZE = 256
MIB = 1 << 20

VM = pl.BlockSpec(memory_space=pltpu.VMEM)
SM = pl.BlockSpec(memory_space=pltpu.SMEM)
ANY = pl.BlockSpec(memory_space=pl.ANY)

PAIR = 2 * CAP
SPARE = 3 * PAIR


def on_chip(x):
    return pltpu.with_memory_space_constraint(x, pltpu.VMEM)


def partners(n_cols):
    i, j = lax.axis_index("gx"), lax.axis_index("gy")
    here = i * n_cols + j
    step_y, step_x = 1 - 2 * (j % 2), 1 - 2 * (i % 2)
    return here, (
        here + step_y,
        here - step_y,
        here + step_x * n_cols,
        here - step_x * n_cols,
    )


def dot(a, b):
    return jnp.dot(a, b, preferred_element_type=F32)


def in_hbm(x):
    return pltpu.with_memory_space_constraint(x, pltpu.HBM)


def in_smem(x):
    return pltpu.with_memory_space_constraint(x, pltpu.SMEM)


def settle(tab, counts, source, slot):
    for p in range(PAIR):
        filled = p % CAP < counts[p // CAP]
        link = jnp.where(filled, tab[p], 0)
        tab[p] = link
        tab[PAIR + p] = source[link]
        tab[2 * PAIR + p] = jnp.where(filled, slot[link] + 1, 0)


def fetch(tab, side, blocks, buf, sems):
    copies = [
        pltpu.make_async_copy(blocks.at[tab[side * CAP + k]], buf.at[k], sems.at[k])
        for k in range(CAP)
    ]
    for copy in copies:
        copy.start(priority=1)
    return copies


def send_terms(tab, block, field, packs, sides=(0, 1)):
    for n, p in enumerate(side * CAP + k for side in sides for k in range(CAP)):
        term = jnp.where(tab[2 * PAIR + p] > 0, dot(block(p), field[tab[PAIR + p]]), 0.0)
        packs[n // CAP][pl.ds((n % CAP) * P_SIZE, P_SIZE), :] = term.astype(BF16)


def clear_tail(pack, used):
    for row in range(used, pack.shape[0], PAD):
        pack[pl.ds(row, PAD), :] = jnp.zeros((PAD, S), BF16)


def put_slots(tab, packs, sides=(0, 1)):
    row = lax.broadcasted_iota(I32, (SLOT_ROWS, S), 0)
    for n, side in enumerate(sides):
        slots = jnp.zeros((SLOT_ROWS, S), I32)
        for k in range(CAP):
            slots = jnp.where(row == k, tab[2 * PAIR + side * CAP + k], slots)
        packs[n][pl.ds(TERM_ROWS, SLOT_ROWS), :] = slots.astype(F32).astype(BF16)


def sensor_rows(cells, weights, weights_sum):
    cell, weight = cells[...], weights[...]
    total = weight
    for shift in range(1, TAPS):
        same = pltpu.roll(cell, shift, 0) == cell
        total = total + jnp.where(same, pltpu.roll(weight, shift, 0), 0.0)
    weights_sum[...] = total
    meta = []
    for part in ((cell >> 7).astype(F32), (cell & 127).astype(F32), total):
        for q in range(SENS // S):
            meta.append(part[:, q * S : (q + 1) * S])
    return jnp.concatenate(meta, axis=0).astype(BF16)


def first_kernel(
    n_cols, target_far, source_far, slot_far, emission, blocks, cells_far, weights_far,
    pack, tab, weights_sum, target, source, slot, field, cells, meta,
    buf, weights, sems, sem_field, sem_links, sem_sensors,
):
    link_copies = [
        pltpu.make_async_copy(far, near, sem_links.at[n])
        for n, (far, near) in enumerate(
            ((target_far, target), (source_far, source), (slot_far, slot))
        )
    ]
    sensor_copies = [
        pltpu.make_async_copy(cells_far, cells, sem_sensors.at[0]),
        pltpu.make_async_copy(weights_far, weights, sem_sensors.at[1]),
    ]
    field_copy = pltpu.make_async_copy(emission, field, sem_field)
    for copy in (*link_copies, field_copy, *sensor_copies):
        copy.start(priority=1)
    gy_e, gy_o, _, _ = partners(n_cols)[1]
    link_copies[0].wait()

    def scan(link, counts):
        owner = target[0, link]
        even, odd = owner == gy_e, owner == gy_o
        tab[jnp.where(even, counts[0], jnp.where(odd, CAP + counts[1], SPARE))] = link
        return counts[0] + even.astype(I32), counts[1] + odd.astype(I32)

    counts = lax.fori_loop(0, LINKS, scan, (jnp.int32(0),) * 2, unroll=24)
    for copy in link_copies[1:]:
        copy.wait()
    settle(tab, counts, source, slot)
    copies = fetch(tab, 1, blocks, buf, sems)
    put_slots(tab, (pack,), (1,))
    for copy in sensor_copies:
        copy.wait()
    rows = sensor_rows(cells, weights, weights_sum)
    meta[...] = rows
    pack[pl.ds(GX_ROWS, META_ROWS), :] = rows
    clear_tail(pack, GY_ROWS)
    field_copy.wait()
    for copy in copies:
        copy.wait()
    send_terms(tab, lambda p: buf[p - CAP], field, (pack,), (1,))


def even_kernel(tab, blocks, field, meta, pack):
    put_slots(tab, (pack,), (0,))
    pack[pl.ds(GX_ROWS, META_ROWS), :] = meta[...]
    send_terms(tab, lambda p: blocks[tab[p]], field, (pack,), (0,))


def even_second_kernel(tab, blocks, field, pack):
    clear_tail(pack, TERM_ROWS)
    send_terms(tab, lambda p: blocks[tab[p]], field, (pack,), (0,))


def gx_kernel(n_cols, target, source, slot, field, blocks, pack_e, pack_o, tab, own):
    gy_e, gy_o, gx_e, gx_o = partners(n_cols)[1]

    def scan(link, counts):
        owner = target[0, link]
        even, odd = owner == gx_e, owner == gx_o
        other = even | odd | (owner == gy_e) | (owner == gy_o)
        tab[jnp.where(even, counts[0], jnp.where(odd, CAP + counts[1], SPARE))] = link
        own[counts[2]] = link
        return (
            counts[0] + even.astype(I32),
            counts[1] + odd.astype(I32),
            counts[2] + jnp.where(other, 0, 1),
        )

    counts = lax.fori_loop(0, LINKS, scan, (jnp.int32(0),) * 3, unroll=24)
    settle(tab, counts, source, slot)
    packs = (pack_e, pack_o)
    put_slots(tab, packs)
    for k in range(GROUP):
        own[counts[2] + k] = 0
    own[OWN_SIZE - 1] = counts[2]
    send_terms(tab, lambda p: blocks[tab[p]], field, packs)


def gx_second_kernel(tab, blocks, field, pack_e, pack_o):
    send_terms(tab, lambda p: blocks[tab[p]], field, (pack_e, pack_o))


def own_terms(own, source, slot, blocks, field, acc):
    acc[...] = jnp.zeros_like(acc)
    count = own[OWN_SIZE - 1]

    def group(first, size):
        terms = []
        for u in range(size):
            link = own[first + u]
            terms.append(dot(blocks[link], field[source[link]]).astype(BF16))
        for u in range(size):
            n = first + u
            acc[jnp.where(n < count, slot[own[n]], CL)] += terms[u].astype(F32)

    def whole(g, _):
        group(g * GROUP, GROUP)
        return 0

    halves = (count + GROUP // 2 - 1) // (GROUP // 2)
    groups = halves // 2
    lax.fori_loop(0, groups, whole, 0)

    @pl.when(halves > 2 * groups)
    def _():
        group(groups * GROUP, GROUP // 2)


def own_first_kernel(own, source, slot, blocks, field, rho, acc, rho_full):
    for q in range(ROWS // S):
        wide = jnp.broadcast_to(rho[pl.ds(q, 1), :], (S, S))
        rho_full[pl.ds(q * S, S), :] = wide.T
    own_terms(own, source, slot, blocks, field, acc)


def own_kernel(own, source, slot, blocks, field, acc):
    own_terms(own, source, slot, blocks, field, acc)


def slots_of(arrived):
    out = []
    for ref in arrived:
        values = ref[pl.ds(TERM_ROWS, SLOT_ROWS), :].astype(F32).astype(I32)
        for k in range(CAP):
            value = values[k, 0]
            out.append(jnp.where(value == 0, CL, value - 1))
    return out


def add_arrived(aims, arrived, acc):
    for n, aim in enumerate(aims):
        rows = pl.ds((n % CAP) * P_SIZE, P_SIZE)
        acc[aim] += arrived[n // CAP][rows, :].astype(F32)


def radiosity_of(emission, rho_full, acc, c):
    return emission[c].astype(F32) + rho_full[pl.ds(c * P_SIZE, P_SIZE), :] * acc[c]


def add_slots_kernel(acc_in, first, second, acc, aims_out):
    del acc_in
    aims = slots_of((first, second))
    for n, aim in enumerate(aims):
        aims_out[n] = aim
    add_arrived(aims, (first, second), acc)


def add_kernel(aims, acc_in, first, second, acc):
    del acc_in
    add_arrived([aims[n] for n in range(PAIR)], (first, second), acc)


def second_kernel(
    tab, blocks, emission, rho_full, acc_in, mix_own, gy_e, gy_o,
    pack, field, aims_out, acc,
):
    del mix_own
    add_slots_kernel(acc_in, gy_e, gy_o, acc, aims_out)
    for c in range(CL):
        field[c] = radiosity_of(emission, rho_full, acc, c).astype(BF16)
    clear_tail(pack, TERM_ROWS)
    send_terms(tab, lambda p: blocks[tab[p]], field, (pack,), (1,))


def spread(cell_rows, weight_rows, out):
    tile, steps = 16, 24
    for q in range(SENS // S):
        cells = [jnp.broadcast_to(cell_rows(k, q), (tile, S)).astype(I16) for k in range(TAPS)]
        weights = [jnp.broadcast_to(weight_rows(k, q), (tile, S)).astype(BF16) for k in range(TAPS)]

        def fill(n, first):
            for m in range(steps):
                here = first + jnp.asarray(m * tile, I16)
                value = jnp.zeros((tile, S), BF16)
                for k in range(TAPS):
                    value = jnp.where(cells[k] == here, weights[k], value)
                start = pl.multiple_of((n * steps + m) * tile, tile)
                out[pl.ds(start, tile), pl.ds(q * S, S)] = value
            return first + jnp.asarray(steps * tile, I16)

        first = lax.broadcasted_iota(I32, (tile, S), 0).astype(I16)
        lax.fori_loop(0, ROWS // (steps * tile), fill, first)


def spread_own_kernel(cells, weights, out):
    spread(
        lambda k, q: cells[pl.ds(k, 1), pl.ds(q * S, S)] - ROWS,
        lambda k, q: weights[pl.ds(k, 1), pl.ds(q * S, S)],
        out,
    )


def spread_pair_kernel(n_cols, gy_e, gy_o, out_e, out_o):
    here, (even, odd, _, _) = partners(n_cols)
    blocks = SENS // S * TAPS
    for partner, arrived, out in ((even, gy_e, out_e), (odd, gy_o, out_o)):
        base = jnp.where(partner > here, 0, 2 * ROWS)
        high = arrived[pl.ds(GX_ROWS, blocks), :].astype(F32).astype(I32)
        low = arrived[pl.ds(GX_ROWS + blocks, blocks), :].astype(F32).astype(I32)
        weight = arrived[pl.ds(GX_ROWS + 2 * blocks, blocks), :].astype(F32)
        cell = high * 128 + low - base
        spread(
            lambda k, q: cell[q * TAPS + k : q * TAPS + k + 1, :],
            lambda k, q: weight[q * TAPS + k : q * TAPS + k + 1, :],
            out,
        )


def final_kernel(
    emission, rho_full, aims, acc_in, gy_e, gy_o, mix, radiosity, part, turned, acc
):
    add_kernel(aims, acc_in, gy_e, gy_o, acc)
    for c in range(CL):
        value = radiosity_of(emission, rho_full, acc, c)
        radiosity[pl.ds(c * P_SIZE, P_SIZE), :] = value
        turned[:, pl.ds(c * P_SIZE, P_SIZE)] = value.T.astype(BF16)
    part[...] = dot(turned[...], mix[...]).astype(BF16)


def sensor_kernel(turned, mix, out):
    out[...] = dot(turned[...], mix[...]).astype(out.dtype)


def last_kernel(own, part_e, part_o, out):
    total = own[...] + part_e[...].astype(F32) + part_o[...].astype(F32)
    out[...] = total.T


def swap(x, axis, odd):
    size = lax.axis_size(axis)
    pairs = [(i, i + 1) for i in range(odd, size - 1, 2)]
    return lax.ppermute(x, axis, [p for a, b in pairs for p in ((a, b), (b, a))])


def exchange(axis, even, odd):
    from_odd = swap(odd, axis, 1)
    return [on_chip(swap(even, axis, 0)), on_chip(from_odd)]


def per_device(
    emission, reflectance, link_blocks, link_source, link_target, link_slot, sensor_cell, sensor_weight
):
    n_cols = lax.axis_size("gy")
    sensors_far = in_hbm(sensor_cell.T), in_hbm(sensor_weight.T)
    cube = in_hbm(emission.reshape(CL, P_SIZE, S))
    far, near = in_hbm(link_blocks), on_chip(link_blocks)
    links_far = [in_hbm(x) for x in (link_target.T, link_source, link_slot)]
    field_shape = pltpu.VMEM((CL, P_SIZE, S), BF16)
    acc_shape = pltpu.VMEM((CL + 1, P_SIZE, S), F32)
    mix_shape = pltpu.VMEM((ROWS, SENS), BF16)

    def call(kernel, name, out_shape, in_specs, out_specs, **more):
        return pl.pallas_call(
            kernel,
            out_shape=out_shape,
            in_specs=in_specs,
            out_specs=out_specs,
            compiler_params=pltpu.CompilerParams(vmem_limit_bytes=16 * MIB),
            name=name,
            **more,
        )

    def pack_shape(rows):
        return pltpu.VMEM((rows, S), BF16)

    def table(size):
        return pltpu.SMEM((size,), I32)

    out_gy_o, tab_y, weights_sum, *links, field, cells, meta = call(
        functools.partial(first_kernel, n_cols),
        "gy_odd_terms",
        [pack_shape(GY_ROWS + PAD), table(128), pltpu.VMEM((TAPS, SENS), F32)]
        + [pltpu.SMEM(x.shape, I32) for x in links_far]
        + [field_shape, pltpu.VMEM((TAPS, SENS), I32), pack_shape(META_ROWS)],
        [ANY] * 7,
        [VM, SM, VM, SM, SM, SM, VM, VM, VM],
        scratch_shapes=[
            pltpu.VMEM((CAP, P_SIZE, P_SIZE), BF16),
            pltpu.VMEM((TAPS, SENS), F32),
            pltpu.SemaphoreType.DMA((CAP,)),
            pltpu.SemaphoreType.DMA,
            pltpu.SemaphoreType.DMA((3,)),
            pltpu.SemaphoreType.DMA((2,)),
        ],
    )(*links_far, cube, far, *sensors_far)
    links, tab_y = [in_smem(x) for x in links], in_smem(tab_y)
    emitted = on_chip(field)
    out_gy_e = call(even_kernel, "gy_even_terms", pack_shape(GY_ROWS), [SM, VM, VM, VM], VM)(
        tab_y, near, emitted, on_chip(meta)
    )
    gy_e, gy_o = exchange("gy", out_gy_e, out_gy_o)
    out_gx_e, out_gx_o, tab_x, own = call(
        functools.partial(gx_kernel, n_cols),
        "gx_terms",
        [pack_shape(GX_ROWS)] * 2 + [table(128), table(OWN_SIZE)],
        [SM, SM, SM, VM, VM],
        [VM, VM, SM, SM],
    )(*links, emitted, near)
    tab_x, own = in_smem(tab_x), in_smem(own)
    gx_e, gx_o = exchange("gx", out_gx_e, out_gx_o)
    acc, rho_full = call(
        own_first_kernel,
        "own_first",
        [acc_shape, pltpu.VMEM((ROWS, S), F32)],
        [SM, SM, SM, VM, VM, VM],
        [VM, VM],
    )(own, *links[1:], near, emitted, reflectance.reshape(ROWS // S, S))
    rho_full = on_chip(rho_full)
    mix_own = call(spread_own_kernel, "spread_own", mix_shape, [VM, VM], VM)(
        on_chip(cells), on_chip(weights_sum)
    )
    mix_own = on_chip(mix_own)
    acc, aims_x = call(
        add_slots_kernel,
        "add_gx_first",
        [acc_shape, table(PAIR)],
        [VM] * 3,
        [VM, SM],
        input_output_aliases={0: 0},
    )(on_chip(acc), gx_e, gx_o)

    out_gy_o, field, aims_y, _ = call(
        second_kernel,
        "gy_odd_second",
        [pack_shape(TERM_ROWS + 2 * PAD), field_shape, table(PAIR), acc_shape],
        [SM, VM, VM, VM, VM, ANY, VM, VM],
        [VM, VM, SM, VM],
        input_output_aliases={4: 3},
    )(tab_y, near, emitted, rho_full, on_chip(acc), mix_own, gy_e, gy_o)
    field = on_chip(field)
    mix_e, mix_o = call(
        functools.partial(spread_pair_kernel, n_cols), "spread_pair", [mix_shape] * 2, [VM, VM], [VM, VM]
    )(gy_e, gy_o)
    out_gy_e = call(
        even_second_kernel, "gy_even_second", pack_shape(TERM_ROWS + PAD), [SM, VM, VM], VM
    )(tab_y, near, field)
    gy_e, gy_o = exchange("gy", out_gy_e, out_gy_o)
    sent = call(
        gx_second_kernel, "gx_second", [pack_shape(TERM_ROWS)] * 2, [SM, VM, VM], [VM, VM]
    )(tab_x, near, field)
    gx_e, gx_o = exchange("gx", *sent)
    acc = call(own_kernel, "own_second", acc_shape, [SM, SM, SM, VM, VM], VM)(
        own, *links[1:], near, field
    )
    acc = call(
        add_kernel, "add_gx_second", acc_shape, [SM, VM, VM, VM], VM, input_output_aliases={1: 0}
    )(in_smem(aims_x), on_chip(acc), gx_e, gx_o)

    radiosity, part_o, turned, _ = call(
        final_kernel,
        "final_sum",
        [pltpu.VMEM((ROWS, S), F32), pltpu.VMEM((S, SENS), BF16), pltpu.VMEM((S, ROWS), BF16), acc_shape],
        [VM, VM, SM, VM, VM, VM, VM],
        [VM] * 4,
        input_output_aliases={3: 3},
    )(emitted, rho_full, in_smem(aims_y), on_chip(acc), gy_e, gy_o, on_chip(mix_o))
    turned = on_chip(turned)

    def sensor_sums(mix, dtype, name):
        out = call(sensor_kernel, name, pltpu.VMEM((S, SENS), dtype), [VM, VM], VM)(turned, mix)
        return on_chip(out)

    from_o = swap(part_o, "gy", 1)
    from_e = swap(sensor_sums(on_chip(mix_e), BF16, "even_sensors"), "gy", 0)
    sensor_values = call(
        last_kernel, "sensor_sum", jax.ShapeDtypeStruct((SENS, S), F32), [VM, VM, VM], VM
    )(sensor_sums(mix_own, F32, "own_sensors"), on_chip(from_e), on_chip(from_o))
    return radiosity, sensor_values


def solution(mesh):
    spread_axes = P(("gx", "gy"))
    rows = P(("gx", "gy"), None)
    return jax.shard_map(
        per_device,
        mesh=mesh,
        in_specs=(rows, spread_axes, P(("gx", "gy"), None, None), spread_axes, rows, spread_axes, rows, rows),
        out_specs=(rows, rows),
        check_vma=False,
    )
```

```python
import functools

import jax
import jax.numpy as jnp
from jax import lax
from jax.experimental import pallas as pl
from jax.experimental.pallas import tpu as pltpu
from jax.sharding import PartitionSpec as P

BF16, F32, I32, I16 = jnp.bfloat16, jnp.float32, jnp.int32, jnp.int16
P_SIZE = 256
S = 128
CL = 12
SENS = 512
TAPS = 8
LINKS = 144
CAP = 9
ROWS = CL * P_SIZE
TERM_ROWS = CAP * P_SIZE
SLOT_ROWS = 16
META_ROWS = 3 * TAPS * SENS // S
GX_ROWS = TERM_ROWS + SLOT_ROWS
GY_ROWS = GX_ROWS + META_ROWS
PAD = 8
TAIL = 8
GROUP = 24
OWN_SIZE = 256
MIB = 1 << 20

VM = pl.BlockSpec(memory_space=pltpu.VMEM)
SM = pl.BlockSpec(memory_space=pltpu.SMEM)
ANY = pl.BlockSpec(memory_space=pl.ANY)

PAIR = 2 * CAP
SPARE = 3 * PAIR


def on_chip(x):
    return pltpu.with_memory_space_constraint(x, pltpu.VMEM)


def partners(n_cols):
    i, j = lax.axis_index("gx"), lax.axis_index("gy")
    here = i * n_cols + j
    step_y, step_x = 1 - 2 * (j % 2), 1 - 2 * (i % 2)
    return here, (
        here + step_y,
        here - step_y,
        here + step_x * n_cols,
        here - step_x * n_cols,
    )


def dot(a, b):
    return jnp.dot(a, b, preferred_element_type=F32)


def in_hbm(x):
    return pltpu.with_memory_space_constraint(x, pltpu.HBM)


def in_smem(x):
    return pltpu.with_memory_space_constraint(x, pltpu.SMEM)


def settle(tab, counts, source, slot):
    for p in range(PAIR):
        filled = p % CAP < counts[p // CAP]
        link = jnp.where(filled, tab[p], 0)
        tab[p] = link
        tab[PAIR + p] = source[link]
        tab[2 * PAIR + p] = jnp.where(filled, slot[link] + 1, 0)


def fetch(tab, side, blocks, buf, sems):
    copies = [
        pltpu.make_async_copy(blocks.at[tab[side * CAP + k]], buf.at[k], sems.at[k])
        for k in range(CAP)
    ]
    for copy in copies:
        copy.start(priority=1)
    return copies


def send_terms(tab, block, field, packs, sides=(0, 1)):
    for n, p in enumerate(side * CAP + k for side in sides for k in range(CAP)):
        term = jnp.where(tab[2 * PAIR + p] > 0, dot(block(p), field[tab[PAIR + p]]), 0.0)
        packs[n // CAP][pl.ds((n % CAP) * P_SIZE, P_SIZE), :] = term.astype(BF16)


def clear_tail(pack, used):
    for row in range(used, pack.shape[0], PAD):
        pack[pl.ds(row, PAD), :] = jnp.zeros((PAD, S), BF16)


def put_slots(tab, packs, sides=(0, 1)):
    row = lax.broadcasted_iota(I32, (SLOT_ROWS, S), 0)
    for n, side in enumerate(sides):
        slots = jnp.zeros((SLOT_ROWS, S), I32)
        for k in range(CAP):
            slots = jnp.where(row == k, tab[2 * PAIR + side * CAP + k], slots)
        packs[n][pl.ds(TERM_ROWS, SLOT_ROWS), :] = slots.astype(F32).astype(BF16)


def sensor_rows(cells, weights, weights_sum):
    cell, weight = cells[...], weights[...]
    total = weight
    for shift in range(1, TAPS):
        same = pltpu.roll(cell, shift, 0) == cell
        total = total + jnp.where(same, pltpu.roll(weight, shift, 0), 0.0)
    weights_sum[...] = total
    meta = []
    for part in ((cell >> 7).astype(F32), (cell & 127).astype(F32), total):
        for q in range(SENS // S):
            meta.append(part[:, q * S : (q + 1) * S])
    return jnp.concatenate(meta, axis=0).astype(BF16)


def first_kernel(
    n_cols, target_far, source_far, slot_far, emission, blocks, cells_far, weights_far,
    pack, tab, weights_sum, target, source, slot, field, cells, meta,
    buf, weights, sems, sem_field, sem_links, sem_sensors,
):
    link_copies = [
        pltpu.make_async_copy(far, near, sem_links.at[n])
        for n, (far, near) in enumerate(
            ((target_far, target), (source_far, source), (slot_far, slot))
        )
    ]
    sensor_copies = [
        pltpu.make_async_copy(cells_far, cells, sem_sensors.at[0]),
        pltpu.make_async_copy(weights_far, weights, sem_sensors.at[1]),
    ]
    field_copy = pltpu.make_async_copy(emission, field, sem_field)
    for copy in (*link_copies, field_copy, *sensor_copies):
        copy.start(priority=1)
    gy_e, gy_o, _, _ = partners(n_cols)[1]
    link_copies[0].wait()

    def scan(link, counts):
        owner = target[0, link]
        even, odd = owner == gy_e, owner == gy_o
        tab[jnp.where(even, counts[0], jnp.where(odd, CAP + counts[1], SPARE))] = link
        return counts[0] + even.astype(I32), counts[1] + odd.astype(I32)

    counts = lax.fori_loop(0, LINKS, scan, (jnp.int32(0),) * 2, unroll=24)
    for copy in link_copies[1:]:
        copy.wait()
    settle(tab, counts, source, slot)
    copies = fetch(tab, 1, blocks, buf, sems)
    put_slots(tab, (pack,), (1,))
    for copy in sensor_copies:
        copy.wait()
    rows = sensor_rows(cells, weights, weights_sum)
    meta[...] = rows
    pack[pl.ds(GX_ROWS, META_ROWS), :] = rows
    clear_tail(pack, GY_ROWS)
    field_copy.wait()
    for copy in copies:
        copy.wait()
    send_terms(tab, lambda p: buf[p - CAP], field, (pack,), (1,))


def even_kernel(tab, blocks, field, meta, pack):
    put_slots(tab, (pack,), (0,))
    pack[pl.ds(GX_ROWS, META_ROWS), :] = meta[...]
    send_terms(tab, lambda p: blocks[tab[p]], field, (pack,), (0,))


def even_second_kernel(tab, blocks, field, pack):
    clear_tail(pack, TERM_ROWS)
    send_terms(tab, lambda p: blocks[tab[p]], field, (pack,), (0,))


def gx_kernel(n_cols, target, source, slot, field, blocks, pack_e, pack_o, tab, own):
    gy_e, gy_o, gx_e, gx_o = partners(n_cols)[1]

    def scan(link, counts):
        owner = target[0, link]
        even, odd = owner == gx_e, owner == gx_o
        other = even | odd | (owner == gy_e) | (owner == gy_o)
        tab[jnp.where(even, counts[0], jnp.where(odd, CAP + counts[1], SPARE))] = link
        own[counts[2]] = link
        return (
            counts[0] + even.astype(I32),
            counts[1] + odd.astype(I32),
            counts[2] + jnp.where(other, 0, 1),
        )

    counts = lax.fori_loop(0, LINKS, scan, (jnp.int32(0),) * 3, unroll=24)
    settle(tab, counts, source, slot)
    packs = (pack_e, pack_o)
    put_slots(tab, packs)
    for k in range(GROUP):
        own[counts[2] + k] = 0
    own[OWN_SIZE - 1] = counts[2]
    send_terms(tab, lambda p: blocks[tab[p]], field, packs)


def gx_second_kernel(tab, blocks, field, pack_e, pack_o):
    send_terms(tab, lambda p: blocks[tab[p]], field, (pack_e, pack_o))


def own_terms(own, source, slot, blocks, field, acc):
    acc[...] = jnp.zeros_like(acc)
    count = own[OWN_SIZE - 1]

    def group(first, size):
        terms = []
        for u in range(size):
            link = own[first + u]
            terms.append(dot(blocks[link], field[source[link]]).astype(BF16))
        for u in range(size):
            n = first + u
            acc[jnp.where(n < count, slot[own[n]], CL)] += terms[u].astype(F32)

    def whole(g, _):
        group(g * GROUP, GROUP)
        return 0

    halves = (count + GROUP // 2 - 1) // (GROUP // 2)
    groups = halves // 2
    lax.fori_loop(0, groups, whole, 0)

    @pl.when(halves > 2 * groups)
    def _():
        group(groups * GROUP, GROUP // 2)


def own_first_kernel(own, source, slot, blocks, field, rho, acc, rho_full):
    for q in range(ROWS // S):
        wide = jnp.broadcast_to(rho[pl.ds(q, 1), :], (S, S))
        rho_full[pl.ds(q * S, S), :] = wide.T
    own_terms(own, source, slot, blocks, field, acc)


def own_kernel(own, source, slot, blocks, field, acc):
    own_terms(own, source, slot, blocks, field, acc)


def slots_of(arrived):
    out = []
    for ref in arrived:
        values = ref[pl.ds(TERM_ROWS, SLOT_ROWS), :].astype(F32).astype(I32)
        for k in range(CAP):
            value = values[k, 0]
            out.append(jnp.where(value == 0, CL, value - 1))
    return out


def add_arrived(aims, arrived, acc):
    for n, aim in enumerate(aims):
        rows = pl.ds((n % CAP) * P_SIZE, P_SIZE)
        acc[aim] += arrived[n // CAP][rows, :].astype(F32)


def radiosity_of(emission, rho_full, acc, c):
    return emission[c].astype(F32) + rho_full[pl.ds(c * P_SIZE, P_SIZE), :] * acc[c]


def add_slots_kernel(acc_in, first, second, acc, aims_out):
    del acc_in
    aims = slots_of((first, second))
    for n, aim in enumerate(aims):
        aims_out[n] = aim
    add_arrived(aims, (first, second), acc)


def add_kernel(aims, acc_in, first, second, acc):
    del acc_in
    add_arrived([aims[n] for n in range(PAIR)], (first, second), acc)


def second_kernel(
    tab, blocks, emission, rho_full, acc_in, mix_own, gy_e, gy_o,
    pack, field, aims_out, acc,
):
    del mix_own
    add_slots_kernel(acc_in, gy_e, gy_o, acc, aims_out)
    for c in range(CL):
        field[c] = radiosity_of(emission, rho_full, acc, c).astype(BF16)
    clear_tail(pack, TERM_ROWS)
    send_terms(tab, lambda p: blocks[tab[p]], field, (pack,), (1,))


def spread(cell_rows, weight_rows, out):
    tile, steps = 16, 24
    for q in range(SENS // S):
        cells = [jnp.broadcast_to(cell_rows(k, q), (tile, S)).astype(I16) for k in range(TAPS)]
        weights = [jnp.broadcast_to(weight_rows(k, q), (tile, S)).astype(BF16) for k in range(TAPS)]

        def fill(n, first):
            for m in range(steps):
                here = first + jnp.asarray(m * tile, I16)
                value = jnp.zeros((tile, S), BF16)
                for k in range(TAPS):
                    value = jnp.where(cells[k] == here, weights[k], value)
                start = pl.multiple_of((n * steps + m) * tile, tile)
                out[pl.ds(start, tile), pl.ds(q * S, S)] = value
            return first + jnp.asarray(steps * tile, I16)

        first = lax.broadcasted_iota(I32, (tile, S), 0).astype(I16)
        lax.fori_loop(0, ROWS // (steps * tile), fill, first)


def spread_own_kernel(cells, weights, out):
    spread(
        lambda k, q: cells[pl.ds(k, 1), pl.ds(q * S, S)] - ROWS,
        lambda k, q: weights[pl.ds(k, 1), pl.ds(q * S, S)],
        out,
    )


def spread_pair_kernel(n_cols, gy_e, gy_o, out_e, out_o):
    here, (even, odd, _, _) = partners(n_cols)
    blocks = SENS // S * TAPS
    for partner, arrived, out in ((even, gy_e, out_e), (odd, gy_o, out_o)):
        base = jnp.where(partner > here, 0, 2 * ROWS)
        high = arrived[pl.ds(GX_ROWS, blocks), :].astype(F32).astype(I32)
        low = arrived[pl.ds(GX_ROWS + blocks, blocks), :].astype(F32).astype(I32)
        weight = arrived[pl.ds(GX_ROWS + 2 * blocks, blocks), :].astype(F32)
        cell = high * 128 + low - base
        spread(
            lambda k, q: cell[q * TAPS + k : q * TAPS + k + 1, :],
            lambda k, q: weight[q * TAPS + k : q * TAPS + k + 1, :],
            out,
        )


def final_kernel(
    emission, rho_full, aims, acc_in, gy_e, gy_o, mix_e, mix_o, radiosity, part_e, part_o, turned, acc
):
    add_kernel(aims, acc_in, gy_e, gy_o, acc)
    for c in range(CL):
        value = radiosity_of(emission, rho_full, acc, c)
        radiosity[pl.ds(c * P_SIZE, P_SIZE), :] = value
        turned[:, pl.ds(c * P_SIZE, P_SIZE)] = value.T.astype(BF16)
    part_o[pl.ds(0, S), :] = dot(turned[...], mix_o[...]).astype(BF16)
    part_o[pl.ds(S, TAIL), :] = jnp.zeros((TAIL, SENS), BF16)
    part_e[...] = dot(turned[...], mix_e[...]).astype(BF16)


def sensor_kernel(turned, mix, out):
    out[...] = dot(turned[...], mix[...])


def last_kernel(own, part_e, part_o, out):
    total = own[...] + part_e[...].astype(F32) + part_o[pl.ds(0, S), :].astype(F32)
    out[...] = total.T


def swap(x, axis, odd):
    size = lax.axis_size(axis)
    pairs = [(i, i + 1) for i in range(odd, size - 1, 2)]
    return lax.ppermute(x, axis, [p for a, b in pairs for p in ((a, b), (b, a))])


def exchange(axis, even, odd):
    from_odd = swap(odd, axis, 1)
    return [on_chip(swap(even, axis, 0)), on_chip(from_odd)]


def per_device(
    emission, reflectance, link_blocks, link_source, link_target, link_slot, sensor_cell, sensor_weight
):
    n_cols = lax.axis_size("gy")
    sensors_far = in_hbm(sensor_cell.T), in_hbm(sensor_weight.T)
    cube = in_hbm(emission.reshape(CL, P_SIZE, S))
    far, near = in_hbm(link_blocks), on_chip(link_blocks)
    links_far = [in_hbm(x) for x in (link_target.T, link_source, link_slot)]
    field_shape = pltpu.VMEM((CL, P_SIZE, S), BF16)
    acc_shape = pltpu.VMEM((CL + 1, P_SIZE, S), F32)
    mix_shape = pltpu.VMEM((ROWS, SENS), BF16)

    def call(kernel, name, out_shape, in_specs, out_specs, **more):
        return pl.pallas_call(
            kernel,
            out_shape=out_shape,
            in_specs=in_specs,
            out_specs=out_specs,
            compiler_params=pltpu.CompilerParams(vmem_limit_bytes=16 * MIB),
            name=name,
            **more,
        )

    def pack_shape(rows):
        return pltpu.VMEM((rows, S), BF16)

    def table(size):
        return pltpu.SMEM((size,), I32)

    out_gy_o, tab_y, weights_sum, *links, field, cells, meta = call(
        functools.partial(first_kernel, n_cols),
        "gy_odd_terms",
        [pack_shape(GY_ROWS + PAD), table(128), pltpu.VMEM((TAPS, SENS), F32)]
        + [pltpu.SMEM(x.shape, I32) for x in links_far]
        + [field_shape, pltpu.VMEM((TAPS, SENS), I32), pack_shape(META_ROWS)],
        [ANY] * 7,
        [VM, SM, VM, SM, SM, SM, VM, VM, VM],
        scratch_shapes=[
            pltpu.VMEM((CAP, P_SIZE, P_SIZE), BF16),
            pltpu.VMEM((TAPS, SENS), F32),
            pltpu.SemaphoreType.DMA((CAP,)),
            pltpu.SemaphoreType.DMA,
            pltpu.SemaphoreType.DMA((3,)),
            pltpu.SemaphoreType.DMA((2,)),
        ],
    )(*links_far, cube, far, *sensors_far)
    links, tab_y = [in_smem(x) for x in links], in_smem(tab_y)
    emitted = on_chip(field)
    out_gy_e = call(even_kernel, "gy_even_terms", pack_shape(GY_ROWS), [SM, VM, VM, VM], VM)(
        tab_y, near, emitted, on_chip(meta)
    )
    gy_e, gy_o = exchange("gy", out_gy_e, out_gy_o)
    out_gx_e, out_gx_o, tab_x, own = call(
        functools.partial(gx_kernel, n_cols),
        "gx_terms",
        [pack_shape(GX_ROWS)] * 2 + [table(128), table(OWN_SIZE)],
        [SM, SM, SM, VM, VM],
        [VM, VM, SM, SM],
    )(*links, emitted, near)
    tab_x, own = in_smem(tab_x), in_smem(own)
    gx_e, gx_o = exchange("gx", out_gx_e, out_gx_o)
    acc, rho_full = call(
        own_first_kernel,
        "own_first",
        [acc_shape, pltpu.VMEM((ROWS, S), F32)],
        [SM, SM, SM, VM, VM, VM],
        [VM, VM],
    )(own, *links[1:], near, emitted, reflectance.reshape(ROWS // S, S))
    rho_full = on_chip(rho_full)
    mix_own = call(spread_own_kernel, "spread_own", mix_shape, [VM, VM], VM)(
        on_chip(cells), on_chip(weights_sum)
    )
    mix_own = on_chip(mix_own)
    acc, aims_x = call(
        add_slots_kernel,
        "add_gx_first",
        [acc_shape, table(PAIR)],
        [VM] * 3,
        [VM, SM],
        input_output_aliases={0: 0},
    )(on_chip(acc), gx_e, gx_o)

    out_gy_o, field, aims_y, _ = call(
        second_kernel,
        "gy_odd_second",
        [pack_shape(TERM_ROWS + 2 * PAD), field_shape, table(PAIR), acc_shape],
        [SM, VM, VM, VM, VM, ANY, VM, VM],
        [VM, VM, SM, VM],
        input_output_aliases={4: 3},
    )(tab_y, near, emitted, rho_full, on_chip(acc), mix_own, gy_e, gy_o)
    field = on_chip(field)
    mix_e, mix_o = call(
        functools.partial(spread_pair_kernel, n_cols), "spread_pair", [mix_shape] * 2, [VM, VM], [VM, VM]
    )(gy_e, gy_o)
    out_gy_e = call(
        even_second_kernel, "gy_even_second", pack_shape(TERM_ROWS + PAD), [SM, VM, VM], VM
    )(tab_y, near, field)
    gy_e, gy_o = exchange("gy", out_gy_e, out_gy_o)
    sent = call(
        gx_second_kernel, "gx_second", [pack_shape(TERM_ROWS)] * 2, [SM, VM, VM], [VM, VM]
    )(tab_x, near, field)
    gx_e, gx_o = exchange("gx", *sent)
    acc = call(own_kernel, "own_second", acc_shape, [SM, SM, SM, VM, VM], VM)(
        own, *links[1:], near, field
    )
    acc = call(
        add_kernel, "add_gx_second", acc_shape, [SM, VM, VM, VM], VM, input_output_aliases={1: 0}
    )(in_smem(aims_x), on_chip(acc), gx_e, gx_o)

    radiosity, part_e, part_o, turned, _ = call(
        final_kernel,
        "final_sum",
        [
            pltpu.VMEM((ROWS, S), F32),
            pltpu.VMEM((S, SENS), BF16),
            pltpu.VMEM((S + TAIL, SENS), BF16),
            pltpu.VMEM((S, ROWS), BF16),
            acc_shape,
        ],
        [VM, VM, SM] + [VM] * 5,
        [VM] * 5,
        input_output_aliases={3: 4},
    )(emitted, rho_full, in_smem(aims_y), on_chip(acc), gy_e, gy_o, on_chip(mix_e), on_chip(mix_o))
    from_e, from_o = exchange("gy", part_e, part_o)
    own_sum = call(sensor_kernel, "own_sensors", pltpu.VMEM((S, SENS), F32), [VM, VM], VM)(
        on_chip(turned), mix_own
    )
    sensor_values = call(
        last_kernel, "sensor_sum", jax.ShapeDtypeStruct((SENS, S), F32), [VM, VM, VM], VM
    )(on_chip(own_sum), from_e, from_o)
    return radiosity, sensor_values


def solution(mesh):
    spread_axes = P(("gx", "gy"))
    rows = P(("gx", "gy"), None)
    return jax.shard_map(
        per_device,
        mesh=mesh,
        in_specs=(rows, spread_axes, P(("gx", "gy"), None, None), spread_axes, rows, spread_axes, rows, rows),
        out_specs=(rows, rows),
        check_vma=False,
    )
```

```python
import functools

import jax
import jax.numpy as jnp
from jax import lax
from jax.experimental import pallas as pl
from jax.experimental.pallas import tpu as pltpu
from jax.sharding import PartitionSpec as P

BF16, F32, I32, I16 = jnp.bfloat16, jnp.float32, jnp.int32, jnp.int16
P_SIZE = 256
S = 128
CL = 12
SENS = 512
TAPS = 8
LINKS = 144
CAP = 9
ROWS = CL * P_SIZE
TERM_ROWS = CAP * P_SIZE
SLOT_ROWS = 16
META_ROWS = 3 * TAPS * SENS // S
GX_ROWS = TERM_ROWS + SLOT_ROWS
GY_ROWS = GX_ROWS + META_ROWS
PAD = 8
GROUP = 24
OWN_SIZE = 256
MIB = 1 << 20

VM = pl.BlockSpec(memory_space=pltpu.VMEM)
SM = pl.BlockSpec(memory_space=pltpu.SMEM)
ANY = pl.BlockSpec(memory_space=pl.ANY)

PAIR = 2 * CAP
SPARE = 3 * PAIR


def on_chip(x):
    return pltpu.with_memory_space_constraint(x, pltpu.VMEM)


def partners(n_cols):
    i, j = lax.axis_index("gx"), lax.axis_index("gy")
    here = i * n_cols + j
    step_y, step_x = 1 - 2 * (j % 2), 1 - 2 * (i % 2)
    return here, (
        here + step_y,
        here - step_y,
        here + step_x * n_cols,
        here - step_x * n_cols,
    )


def dot(a, b):
    return jnp.dot(a, b, preferred_element_type=F32)


def in_hbm(x):
    return pltpu.with_memory_space_constraint(x, pltpu.HBM)


def in_smem(x):
    return pltpu.with_memory_space_constraint(x, pltpu.SMEM)


def settle(tab, counts, source, slot):
    for p in range(PAIR):
        filled = p % CAP < counts[p // CAP]
        link = jnp.where(filled, tab[p], 0)
        tab[p] = link
        tab[PAIR + p] = source[link]
        tab[2 * PAIR + p] = jnp.where(filled, slot[link] + 1, 0)


def fetch(tab, side, blocks, buf, sems):
    copies = [
        pltpu.make_async_copy(blocks.at[tab[side * CAP + k]], buf.at[k], sems.at[k])
        for k in range(CAP)
    ]
    for copy in copies:
        copy.start(priority=1)
    return copies


def send_terms(tab, block, field, packs, sides=(0, 1)):
    for n, p in enumerate(side * CAP + k for side in sides for k in range(CAP)):
        term = jnp.where(tab[2 * PAIR + p] > 0, dot(block(p), field[tab[PAIR + p]]), 0.0)
        packs[n // CAP][pl.ds((n % CAP) * P_SIZE, P_SIZE), :] = term.astype(BF16)


def clear_tail(pack, used):
    for row in range(used, pack.shape[0], PAD):
        pack[pl.ds(row, PAD), :] = jnp.zeros((PAD, S), BF16)


def put_slots(tab, packs, sides=(0, 1)):
    row = lax.broadcasted_iota(I32, (SLOT_ROWS, S), 0)
    for n, side in enumerate(sides):
        slots = jnp.zeros((SLOT_ROWS, S), I32)
        for k in range(CAP):
            slots = jnp.where(row == k, tab[2 * PAIR + side * CAP + k], slots)
        packs[n][pl.ds(TERM_ROWS, SLOT_ROWS), :] = slots.astype(F32).astype(BF16)


def sensor_rows(cells, weights, weights_sum):
    cell, weight = cells[...], weights[...]
    total = weight
    for shift in range(1, TAPS):
        same = pltpu.roll(cell, shift, 0) == cell
        total = total + jnp.where(same, pltpu.roll(weight, shift, 0), 0.0)
    weights_sum[...] = total
    meta = []
    for part in ((cell >> 7).astype(F32), (cell & 127).astype(F32), total):
        for q in range(SENS // S):
            meta.append(part[:, q * S : (q + 1) * S])
    return jnp.concatenate(meta, axis=0).astype(BF16)


def first_kernel(
    n_cols, target_far, source_far, slot_far, emission, blocks, cells_far, weights_far,
    pack, tab, weights_sum, target, source, slot, field, cells, meta,
    buf, weights, sems, sem_field, sem_links, sem_sensors,
):
    link_copies = [
        pltpu.make_async_copy(far, near, sem_links.at[n])
        for n, (far, near) in enumerate(
            ((target_far, target), (source_far, source), (slot_far, slot))
        )
    ]
    sensor_copies = [
        pltpu.make_async_copy(cells_far, cells, sem_sensors.at[0]),
        pltpu.make_async_copy(weights_far, weights, sem_sensors.at[1]),
    ]
    field_copy = pltpu.make_async_copy(emission, field, sem_field)
    for copy in (*link_copies, field_copy, *sensor_copies):
        copy.start(priority=1)
    gy_e, gy_o, _, _ = partners(n_cols)[1]
    link_copies[0].wait()

    def scan(link, counts):
        owner = target[0, link]
        even, odd = owner == gy_e, owner == gy_o
        tab[jnp.where(even, counts[0], jnp.where(odd, CAP + counts[1], SPARE))] = link
        return counts[0] + even.astype(I32), counts[1] + odd.astype(I32)

    counts = lax.fori_loop(0, LINKS, scan, (jnp.int32(0),) * 2, unroll=24)
    for copy in link_copies[1:]:
        copy.wait()
    settle(tab, counts, source, slot)
    copies = fetch(tab, 1, blocks, buf, sems)
    put_slots(tab, (pack,), (1,))
    for copy in sensor_copies:
        copy.wait()
    rows = sensor_rows(cells, weights, weights_sum)
    meta[...] = rows
    pack[pl.ds(GX_ROWS, META_ROWS), :] = rows
    clear_tail(pack, GY_ROWS)
    field_copy.wait()
    for copy in copies:
        copy.wait()
    send_terms(tab, lambda p: buf[p - CAP], field, (pack,), (1,))


def even_kernel(tab, blocks, field, meta, pack):
    put_slots(tab, (pack,), (0,))
    pack[pl.ds(GX_ROWS, META_ROWS), :] = meta[...]
    send_terms(tab, lambda p: blocks[tab[p]], field, (pack,), (0,))


def even_second_kernel(tab, blocks, field, pack):
    clear_tail(pack, TERM_ROWS)
    send_terms(tab, lambda p: blocks[tab[p]], field, (pack,), (0,))


def gx_kernel(n_cols, target, source, slot, field, blocks, pack_e, pack_o, tab, own):
    gy_e, gy_o, gx_e, gx_o = partners(n_cols)[1]

    def scan(link, counts):
        owner = target[0, link]
        even, odd = owner == gx_e, owner == gx_o
        other = even | odd | (owner == gy_e) | (owner == gy_o)
        tab[jnp.where(even, counts[0], jnp.where(odd, CAP + counts[1], SPARE))] = link
        own[counts[2]] = link
        return (
            counts[0] + even.astype(I32),
            counts[1] + odd.astype(I32),
            counts[2] + jnp.where(other, 0, 1),
        )

    counts = lax.fori_loop(0, LINKS, scan, (jnp.int32(0),) * 3, unroll=24)
    settle(tab, counts, source, slot)
    packs = (pack_e, pack_o)
    put_slots(tab, packs)
    for k in range(GROUP):
        own[counts[2] + k] = 0
    own[OWN_SIZE - 1] = counts[2]
    send_terms(tab, lambda p: blocks[tab[p]], field, packs)


def gx_second_kernel(tab, blocks, field, pack_e, pack_o):
    send_terms(tab, lambda p: blocks[tab[p]], field, (pack_e, pack_o))


def own_terms(own, source, slot, blocks, field, acc):
    acc[...] = jnp.zeros_like(acc)
    count = own[OWN_SIZE - 1]

    def group(first, size):
        terms = []
        for u in range(size):
            link = own[first + u]
            terms.append(dot(blocks[link], field[source[link]]).astype(BF16))
        for u in range(size):
            n = first + u
            acc[jnp.where(n < count, slot[own[n]], CL)] += terms[u].astype(F32)

    def whole(g, _):
        group(g * GROUP, GROUP)
        return 0

    halves = (count + GROUP // 2 - 1) // (GROUP // 2)
    groups = halves // 2
    lax.fori_loop(0, groups, whole, 0)

    @pl.when(halves > 2 * groups)
    def _():
        group(groups * GROUP, GROUP // 2)


def own_first_kernel(own, source, slot, blocks, field, rho, acc, rho_full):
    for q in range(ROWS // S):
        wide = jnp.broadcast_to(rho[pl.ds(q, 1), :], (S, S))
        rho_full[pl.ds(q * S, S), :] = wide.T
    own_terms(own, source, slot, blocks, field, acc)


def own_kernel(own, source, slot, blocks, field, acc):
    own_terms(own, source, slot, blocks, field, acc)


def slots_of(arrived):
    out = []
    for ref in arrived:
        values = ref[pl.ds(TERM_ROWS, SLOT_ROWS), :].astype(F32).astype(I32)
        for k in range(CAP):
            value = values[k, 0]
            out.append(jnp.where(value == 0, CL, value - 1))
    return out


def add_arrived(aims, arrived, acc):
    for n, aim in enumerate(aims):
        rows = pl.ds((n % CAP) * P_SIZE, P_SIZE)
        acc[aim] += arrived[n // CAP][rows, :].astype(F32)


def radiosity_of(emission, rho_full, acc, c):
    return emission[c].astype(F32) + rho_full[pl.ds(c * P_SIZE, P_SIZE), :] * acc[c]


def add_slots_kernel(acc_in, first, second, acc, aims_out):
    del acc_in
    aims = slots_of((first, second))
    for n, aim in enumerate(aims):
        aims_out[n] = aim
    add_arrived(aims, (first, second), acc)


def add_kernel(aims, acc_in, first, second, acc):
    del acc_in
    add_arrived([aims[n] for n in range(PAIR)], (first, second), acc)


def second_kernel(
    tab, blocks, emission, rho_full, acc_in, mix_own, gy_e, gy_o,
    pack, field, aims_out, acc,
):
    del mix_own
    add_slots_kernel(acc_in, gy_e, gy_o, acc, aims_out)
    for c in range(CL):
        field[c] = radiosity_of(emission, rho_full, acc, c).astype(BF16)
    clear_tail(pack, TERM_ROWS)
    send_terms(tab, lambda p: blocks[tab[p]], field, (pack,), (1,))


def spread(cell_rows, weight_rows, out):
    tile, steps = 16, 24
    for q in range(SENS // S):
        cells = [jnp.broadcast_to(cell_rows(k, q), (tile, S)).astype(I16) for k in range(TAPS)]
        weights = [jnp.broadcast_to(weight_rows(k, q), (tile, S)).astype(BF16) for k in range(TAPS)]

        def fill(n, first):
            for m in range(steps):
                here = first + jnp.asarray(m * tile, I16)
                value = jnp.zeros((tile, S), BF16)
                for k in range(TAPS):
                    value = jnp.where(cells[k] == here, weights[k], value)
                start = pl.multiple_of((n * steps + m) * tile, tile)
                out[pl.ds(start, tile), pl.ds(q * S, S)] = value
            return first + jnp.asarray(steps * tile, I16)

        first = lax.broadcasted_iota(I32, (tile, S), 0).astype(I16)
        lax.fori_loop(0, ROWS // (steps * tile), fill, first)


def spread_own_kernel(cells, weights, out):
    spread(
        lambda k, q: cells[pl.ds(k, 1), pl.ds(q * S, S)] - ROWS,
        lambda k, q: weights[pl.ds(k, 1), pl.ds(q * S, S)],
        out,
    )


def spread_pair_kernel(n_cols, gy_e, gy_o, out_e, out_o):
    here, (even, odd, _, _) = partners(n_cols)
    blocks = SENS // S * TAPS
    for partner, arrived, out in ((even, gy_e, out_e), (odd, gy_o, out_o)):
        base = jnp.where(partner > here, 0, 2 * ROWS)
        high = arrived[pl.ds(GX_ROWS, blocks), :].astype(F32).astype(I32)
        low = arrived[pl.ds(GX_ROWS + blocks, blocks), :].astype(F32).astype(I32)
        weight = arrived[pl.ds(GX_ROWS + 2 * blocks, blocks), :].astype(F32)
        cell = high * 128 + low - base
        spread(
            lambda k, q: cell[q * TAPS + k : q * TAPS + k + 1, :],
            lambda k, q: weight[q * TAPS + k : q * TAPS + k + 1, :],
            out,
        )


def final_kernel(
    emission, rho_full, aims, acc_in, gy_e, gy_o, mix, radiosity, part, turned, acc
):
    add_kernel(aims, acc_in, gy_e, gy_o, acc)
    for c in range(CL):
        value = radiosity_of(emission, rho_full, acc, c)
        radiosity[pl.ds(c * P_SIZE, P_SIZE), :] = value
        turned[:, pl.ds(c * P_SIZE, P_SIZE)] = value.T.astype(BF16)
    part[...] = dot(turned[...], mix[...]).astype(BF16)


def sensor_kernel(turned, mix, out):
    out[...] = dot(turned[...], mix[...]).astype(out.dtype)


def last_kernel(own, part_e, part_o, out):
    total = own[...] + part_e[...].astype(F32) + part_o[...].astype(F32)
    out[...] = total.T


def swap(x, axis, odd):
    size = lax.axis_size(axis)
    pairs = [(i, i + 1) for i in range(odd, size - 1, 2)]
    return lax.ppermute(x, axis, [p for a, b in pairs for p in ((a, b), (b, a))])


def exchange(axis, even, odd):
    from_odd = swap(odd, axis, 1)
    return [on_chip(swap(even, axis, 0)), on_chip(from_odd)]


def per_device(
    emission, reflectance, link_blocks, link_source, link_target, link_slot, sensor_cell, sensor_weight
):
    n_cols = lax.axis_size("gy")
    sensors_far = in_hbm(sensor_cell.T), in_hbm(sensor_weight.T)
    cube = in_hbm(emission.reshape(CL, P_SIZE, S))
    far, near = in_hbm(link_blocks), on_chip(link_blocks)
    links_far = [in_hbm(x) for x in (link_target.T, link_source, link_slot)]
    field_shape = pltpu.VMEM((CL, P_SIZE, S), BF16)
    acc_shape = pltpu.VMEM((CL + 1, P_SIZE, S), F32)
    mix_shape = pltpu.VMEM((ROWS, SENS), BF16)

    def call(kernel, name, out_shape, in_specs, out_specs, **more):
        return pl.pallas_call(
            kernel,
            out_shape=out_shape,
            in_specs=in_specs,
            out_specs=out_specs,
            compiler_params=pltpu.CompilerParams(vmem_limit_bytes=16 * MIB),
            name=name,
            **more,
        )

    def pack_shape(rows):
        return pltpu.VMEM((rows, S), BF16)

    def table(size):
        return pltpu.SMEM((size,), I32)

    out_gy_o, tab_y, weights_sum, *links, field, cells, meta = call(
        functools.partial(first_kernel, n_cols),
        "gy_odd_terms",
        [pack_shape(GY_ROWS + PAD), table(128), pltpu.VMEM((TAPS, SENS), F32)]
        + [pltpu.SMEM(x.shape, I32) for x in links_far]
        + [field_shape, pltpu.VMEM((TAPS, SENS), I32), pack_shape(META_ROWS)],
        [ANY] * 7,
        [VM, SM, VM, SM, SM, SM, VM, VM, VM],
        scratch_shapes=[
            pltpu.VMEM((CAP, P_SIZE, P_SIZE), BF16),
            pltpu.VMEM((TAPS, SENS), F32),
            pltpu.SemaphoreType.DMA((CAP,)),
            pltpu.SemaphoreType.DMA,
            pltpu.SemaphoreType.DMA((3,)),
            pltpu.SemaphoreType.DMA((2,)),
        ],
    )(*links_far, cube, far, *sensors_far)
    links, tab_y = [in_smem(x) for x in links], in_smem(tab_y)
    emitted = on_chip(field)
    out_gy_e = call(even_kernel, "gy_even_terms", pack_shape(GY_ROWS), [SM, VM, VM, VM], VM)(
        tab_y, near, emitted, on_chip(meta)
    )
    gy_e, gy_o = exchange("gy", out_gy_e, out_gy_o)
    out_gx_e, out_gx_o, tab_x, own = call(
        functools.partial(gx_kernel, n_cols),
        "gx_terms",
        [pack_shape(GX_ROWS)] * 2 + [table(128), table(OWN_SIZE)],
        [SM, SM, SM, VM, VM],
        [VM, VM, SM, SM],
    )(*links, emitted, near)
    tab_x, own = in_smem(tab_x), in_smem(own)
    gx_e, gx_o = exchange("gx", out_gx_e, out_gx_o)
    acc, rho_full = call(
        own_first_kernel,
        "own_first",
        [acc_shape, pltpu.VMEM((ROWS, S), F32)],
        [SM, SM, SM, VM, VM, VM],
        [VM, VM],
    )(own, *links[1:], near, emitted, reflectance.reshape(ROWS // S, S))
    rho_full = on_chip(rho_full)
    mix_own = call(spread_own_kernel, "spread_own", mix_shape, [VM, VM], VM)(
        on_chip(cells), on_chip(weights_sum)
    )
    mix_own = on_chip(mix_own)
    acc, aims_x = call(
        add_slots_kernel,
        "add_gx_first",
        [acc_shape, table(PAIR)],
        [VM] * 3,
        [VM, SM],
        input_output_aliases={0: 0},
    )(on_chip(acc), gx_e, gx_o)

    out_gy_o, field, aims_y, _ = call(
        second_kernel,
        "gy_odd_second",
        [pack_shape(TERM_ROWS + 2 * PAD), field_shape, table(PAIR), acc_shape],
        [SM, VM, VM, VM, VM, ANY, VM, VM],
        [VM, VM, SM, VM],
        input_output_aliases={4: 3},
    )(tab_y, near, emitted, rho_full, on_chip(acc), mix_own, gy_e, gy_o)
    field = on_chip(field)
    mix_e, mix_o = call(
        functools.partial(spread_pair_kernel, n_cols), "spread_pair", [mix_shape] * 2, [VM, VM], [VM, VM]
    )(gy_e, gy_o)
    out_gy_e = call(
        even_second_kernel, "gy_even_second", pack_shape(TERM_ROWS + PAD), [SM, VM, VM], VM
    )(tab_y, near, field)
    gy_e, gy_o = exchange("gy", out_gy_e, out_gy_o)
    sent = call(
        gx_second_kernel, "gx_second", [pack_shape(TERM_ROWS)] * 2, [SM, VM, VM], [VM, VM]
    )(tab_x, near, field)
    gx_e, gx_o = exchange("gx", *sent)
    acc = call(own_kernel, "own_second", acc_shape, [SM, SM, SM, VM, VM], VM)(
        own, *links[1:], near, field
    )
    acc = call(
        add_kernel, "add_gx_second", acc_shape, [SM, VM, VM, VM], VM, input_output_aliases={1: 0}
    )(in_smem(aims_x), on_chip(acc), gx_e, gx_o)

    radiosity, part_o, turned, _ = call(
        final_kernel,
        "final_sum",
        [pltpu.VMEM((ROWS, S), F32), pltpu.VMEM((S, SENS), BF16), pltpu.VMEM((S, ROWS), BF16), acc_shape],
        [VM, VM, SM, VM, VM, VM, VM],
        [VM] * 4,
        input_output_aliases={3: 3},
    )(emitted, rho_full, in_smem(aims_y), on_chip(acc), gy_e, gy_o, on_chip(mix_o))
    turned = on_chip(turned)

    def sensor_sums(mix, dtype, name):
        out = call(sensor_kernel, name, pltpu.VMEM((S, SENS), dtype), [VM, VM], VM)(turned, mix)
        return on_chip(out)

    from_o = swap(part_o, "gy", 1)
    from_e = swap(sensor_sums(on_chip(mix_e), BF16, "even_sensors"), "gy", 0)
    sensor_values = call(
        last_kernel, "sensor_sum", jax.ShapeDtypeStruct((SENS, S), F32), [VM, VM, VM], VM
    )(sensor_sums(mix_own, F32, "own_sensors"), on_chip(from_e), on_chip(from_o))
    return radiosity, sensor_values


def solution(mesh):
    spread_axes = P(("gx", "gy"))
    rows = P(("gx", "gy"), None)
    return jax.shard_map(
        per_device,
        mesh=mesh,
        in_specs=(rows, spread_axes, P(("gx", "gy"), None, None), spread_axes, rows, spread_axes, rows, rows),
        out_specs=(rows, rows),
        check_vma=False,
    )
```
